256 devices in a mesh: tm: 64 (over x, z, y_lo), tile: 4 (over y_hi, core).
Axes of the slice: x: 4, y: 4 (y_hi: 2, y_lo: 2; y = y_hi * 2 + y_lo), z: 8, core: 2. Of those that a mesh axis runs over, the one named last changes fastest.
Arguments:
- frames: bfloat16 [4096, 8192], P('tm', 'tile')
- partner: int32 [4096], replicated, may hold values from 0 to 4095, as said below
- usable: int32 [4096], replicated, may hold values from 0 to 1, as said below
Outputs:
- cov_inst: float32 [8192, 8192], P('tile', 'tm')
- cov_lag: float32 [8192, 8192], P('tile', 'tm')
The draws below stay inside these ranges and needn't reach their ends.
Inputs may be any that keep to these rules, and one draw needn't show every extreme that they name: partner[t] is either t itself or a frame of the same trajectory 1 to 16 frames after t; the offset 16 occurs in every draw. usable[t] is 1 only where partner[t] > t.
All inputs are finite; a program needn't handle non-finite values.
Results may differ from the reference program's by a relative error of at most 0.0005.
The reference program's roundings to bfloat16 on the way count: a program that leaves them out, or rounds other values in their place, can miss the bound.
Values may be sent and summed in bfloat16 or wider, within the bound.
A program may use at most 64 MiB of HBM per device.

```python
import math
import jax
import jax.numpy as jnp
from jax import lax

FEATURES = 8192
LAG_FRAMES = 16
FRAMES = 4096


def trajectory(key):
    start_key = jax.random.fold_in(key, 101)
    start_flags = jax.random.randint(start_key, (FRAMES,), 0, FRAMES) < 8
    positions = jnp.arange(FRAMES, dtype=jnp.int32)
    early_frame = positions <= LAG_FRAMES
    starts = jnp.where(positions == 0, 1, jnp.where(early_frame, 0, start_flags.astype(jnp.int32)))
    segment = jnp.cumsum(starts) - 1
    full_stride = jax.random.randint(jax.random.fold_in(key, 404), (FRAMES,), 0, 2) == 0
    short_stride = jax.random.randint(jax.random.fold_in(key, 405), (FRAMES,), 1, max(LAG_FRAMES, 2))
    stride = jnp.where(full_stride | (positions == 0), LAG_FRAMES, jnp.minimum(short_stride, LAG_FRAMES))
    target = positions + stride
    forward = jnp.minimum(target, FRAMES - 1)
    inside = (segment[forward] == segment) & (target < FRAMES)
    return (segment, target, positions, inside)


def draw_partner(key, part):
    segment, target, positions, inside = trajectory(key)
    return jnp.where(inside, target, positions).astype(jnp.int32)


def draw_usable(key, part):
    segment, target, positions, inside = trajectory(key)
    kept_frame = jax.random.randint(jax.random.fold_in(key, 202), (FRAMES,), 0, 8) != 0
    return (inside & kept_frame).astype(jnp.int32)


def draw_frames(key, part):
    segment, target, positions, inside = trajectory(key)
    subkeys = jax.random.split(jax.random.fold_in(key, 303), 5)
    offset_base = jax.random.uniform(subkeys[0], (FEATURES,), jnp.float32, 1.0, 4.0)
    amplitude = jnp.exp(jax.random.uniform(subkeys[1], (FEATURES,), jnp.float32, math.log(0.2), 0.0))
    spread_scale = jnp.exp(jax.random.uniform(subkeys[2], (FEATURES,), jnp.float32, math.log(0.3), math.log(3.0)))
    traj_table = jax.random.normal(subkeys[3], (64, FEATURES), jnp.float32)
    jitter = jax.random.normal(subkeys[4], (FRAMES, FEATURES), jnp.float32)
    shifts = traj_table[segment % 64]
    values = offset_base[None, :] + amplitude[None, :] * shifts + spread_scale[None, :] * jitter
    return values.astype(jnp.bfloat16)


def setup_inputs(seed: int = 0) -> dict:
    seeds = jax.random.split(jax.random.key(seed), 4)
    frames = draw_frames(jax.random.fold_in(seeds[3], 71), 0)
    partner = draw_partner(jax.random.fold_in(seeds[3], 71), 0)
    usable = draw_usable(jax.random.fold_in(seeds[3], 71), 0)
    return {"frames": frames, "partner": partner, "usable": usable}


def reference(frames, partner, usable):
    weight = usable.astype(jnp.float32)
    weight_half = usable.astype(jnp.bfloat16)
    frame_count = jnp.sum(weight)
    mean_now = jnp.dot(weight_half[None, :], frames, preferred_element_type=jnp.float32)[0] / frame_count
    lagged = jnp.take(frames, partner, axis=0)
    mean_lag = jnp.dot(weight_half[None, :], lagged, preferred_element_type=jnp.float32)[0] / frame_count
    centered = (frames.astype(jnp.float32) - mean_now[None, :]).astype(jnp.bfloat16)
    columns = (weight[:, None] * (frames.astype(jnp.float32) - mean_now[None, :])).astype(jnp.bfloat16)
    lag_columns = (weight[:, None] * (lagged.astype(jnp.float32) - mean_lag[None, :])).astype(jnp.bfloat16)
    left_side = centered.astype(jnp.float32).T
    cov_inst = jnp.dot(left_side, columns.astype(jnp.float32), precision=lax.Precision.HIGHEST) / frame_count
    cov_lag = jnp.dot(left_side, lag_columns.astype(jnp.float32), precision=lax.Precision.HIGHEST) / frame_count
    return cov_inst, cov_lag
```

```python
import jax
import jax.numpy as jnp
from jax import lax
from jax.experimental import pallas as pl
from jax.experimental.pallas import tpu as pltpu
from jax.sharding import PartitionSpec as P

MESH = pl.DeviceIdType.MESH
NX, NZ, NL = 4, 8, 2
CHUNKS = 4
W = 128


def coords():
    tm, tile = lax.axis_index("tm"), lax.axis_index("tile")
    return tm // (NZ * NL), (tm // NL) % NZ, tm % NL, tile // 2, tile % 2


def device(x, z, yl, yh, c):
    return (x * (NZ * NL) + z * NL + yl, yh * 2 + c)


def kernel(
    partner_ref, usable_ref, frames_ref, inst_ref, lag_ref,
    row, ul, rt, wcol, outb, stat,
    ra_s, ra_r, ca_s, ca_r, own_sem, ring_s, ring_r, cx_s, cx_r, cy_s, cy_r, cc_s, cc_r, out_s, out_r, keep_sem,
):
    x, z, yl, yh, c = coords()
    tile = yh * 2 + c
    nblk = NX * NZ

    peers = []
    for dx in range(NX):
        for dy in range(NL):
            if dx or dy:
                peers.append(device((x + dx) % NX, z, (yl + dy) % NL, yh, c))
    for dz in range(1, NZ):
        for dy in range(NL):
            peers.append(device(x, (z + dz) % NZ, (yl + dy) % NL, yh, c))
    peers.append(device(x, z, yl, 1 - yh, c))
    peers.append(device(x, z, yl, yh, 1 - c))
    barrier = pltpu.get_barrier_semaphore()
    for p in peers:
        pl.semaphore_signal(barrier, inc=1, device_id=p, device_id_type=MESH)

    own_row = pltpu.make_async_copy(
        frames_ref.at[:, pl.ds(pl.multiple_of(x * 512, 512), 512)],
        row.at[x, z, pl.ds(pl.multiple_of(yl * 64, 64), 64), :], own_sem.at[0])
    own_row.start()

    def col_piece(t, start, size):
        return ul.at[pl.ds(start, size), pl.ds(pl.multiple_of(t * W, W), W)]

    my_block = z * NL + yl
    own_col = pltpu.make_async_copy(
        frames_ref.at[:, pl.ds(pl.multiple_of(my_block * W, W), W)],
        col_piece(tile, pl.multiple_of(x * 1024 + my_block * 64, 64), 64), own_sem.at[1])
    own_col.start()

    pl.semaphore_wait(barrier, len(peers))

    row_a2a = []
    for dx in range(NX):
        for dy in range(NL):
            if dx or dy:
                k = dx * NL + dy
                tx = (x + dx) % NX
                cp = pltpu.make_async_remote_copy(
                    src_ref=frames_ref.at[:, pl.ds(pl.multiple_of(tx * 512, 512), 512)],
                    dst_ref=row.at[x, z, pl.ds(pl.multiple_of(yl * 64, 64), 64), :],
                    send_sem=ra_s.at[k], recv_sem=ra_r.at[k],
                    device_id=device(tx, z, (yl + dy) % NL, yh, c), device_id_type=MESH)
                cp.start()
                row_a2a.append(cp)
    col_a2a = []
    for dz in range(NZ):
        for dy in range(NL):
            if dz or dy:
                k = dz * NL + dy
                tz, ty = (z + dz) % NZ, (yl + dy) % NL
                cp = pltpu.make_async_remote_copy(
                    src_ref=frames_ref.at[:, pl.ds(pl.multiple_of((tz * NL + ty) * W, W), W)],
                    dst_ref=col_piece(tile, pl.multiple_of(x * 1024 + my_block * 64, 64), 64),
                    send_sem=ca_s.at[k], recv_sem=ca_r.at[k],
                    device_id=device(x, tz, ty, yh, c), device_id_type=MESH)
                cp.start()
                col_a2a.append(cp)

    total = jnp.sum(usable_ref[...].astype(jnp.float32))

    def weights(i, _):
        w = usable_ref[pl.ds(i, 1), :].astype(jnp.float32)
        wcol[pl.ds(pl.multiple_of(i * W, W), W), :] = jnp.broadcast_to(w, (W, W)).T
        return 0

    lax.fori_loop(0, nblk, weights, 0)
    ul[pl.ds(4096, W), :] = jnp.zeros((W, 1024), jnp.bfloat16)

    def ring(j, d, h):
        step = 1 if d == 0 else NZ - 1
        blk = (z + (NZ - step) * (h - 1)) % NZ
        ref = row.at[:, blk, :, pl.ds(j * W, W)]
        return pltpu.make_async_remote_copy(
            src_ref=ref, dst_ref=ref, send_sem=ring_s.at[d, j, h - 1], recv_sem=ring_r.at[d, j, h - 1],
            device_id=device(x, (z + step) % NZ, yl, yh, c), device_id_type=MESH)

    def hops(j, d):
        return 4 if j % 2 == d else 3

    own_row.wait()
    for cp in row_a2a:
        cp.wait_recv()
    for j in (0, 1):
        for d in (0, 1):
            ring(j, d, 1).start()

    def ring_step(j, h):
        for d in (0, 1):
            if h <= hops(j, d):
                ring(j, d, h).wait_recv()
                if h < hops(j, d):
                    ring(j, d, h + 1).start()

    def frames_of(k):
        return pl.multiple_of(((x + NX - k) % NX) * 1024, 1024)

    def col_x(dx):
        ref = col_piece(tile, frames_of(0), 1024)
        return pltpu.make_async_remote_copy(
            src_ref=ref, dst_ref=ref, send_sem=cx_s.at[dx], recv_sem=cx_r.at[dx],
            device_id=device((x + dx) % NX, z, yl, yh, c), device_id_type=MESH)

    def col_y(k):
        ref = col_piece(tile, frames_of(k), 1024)
        return pltpu.make_async_remote_copy(
            src_ref=ref, dst_ref=ref, send_sem=cy_s.at[k], recv_sem=cy_r.at[k],
            device_id=device(x, z, yl, 1 - yh, c), device_id_type=MESH)

    def col_c(k, other):
        ref = col_piece(tile if other == 0 else (1 - yh) * 2 + c, frames_of(k), 1024)
        return pltpu.make_async_remote_copy(
            src_ref=ref, dst_ref=ref, send_sem=cc_s.at[other, k], recv_sem=cc_r.at[other, k],
            device_id=device(x, z, yl, yh, 1 - c), device_id_type=MESH)

    own_col.wait()
    for cp in col_a2a:
        cp.wait_recv()
    for dx in (1, 3, 2):
        col_x(dx).start()
    col_y(0).start()
    col_c(0, 0).start()

    def from_x(k):
        col_x(k).wait_recv()
        col_y(k).start()
        col_c(k, 0).start()

    def from_y(k):
        col_y(k).wait_recv()
        col_c(k, 1).start()

    def lag_blocks(lo, hi):
        def body(i, acc):
            base = pl.multiple_of(i * W, W)
            p = partner_ref[pl.ds(i, 1), :] - base
            s = lax.broadcasted_iota(jnp.int32, (2 * W, W), 0)
            pick = jnp.where(s == p, 1.0, 0.0).astype(jnp.bfloat16)
            raw = ul[pl.ds(base, 2 * W), pl.ds(0, 512)]
            lagged = lax.dot_general(pick, raw, (((0,), (0,)), ((), ())), preferred_element_type=jnp.float32)
            ul[pl.ds(base, W), pl.ds(512, 512)] = lagged.astype(jnp.bfloat16)
            w = wcol[pl.ds(base, W), :]
            now = raw[:W].astype(jnp.float32)
            parts = [now[:, k * W:(k + 1) * W] * w for k in range(4)]
            parts += [lagged[:, k * W:(k + 1) * W] * w for k in range(4)]
            prod = jnp.concatenate(parts, axis=1)
            return acc + jnp.sum(prod.reshape(16, 8, 1024), axis=0)

        stat[...] += lax.fori_loop(lo, hi, body, jnp.zeros((8, 1024), jnp.float32))

    def center_blocks(lo, hi, mean):
        def body(i, _):
            sl = pl.ds(pl.multiple_of(i * W, W), W)
            ul[sl, :] = (ul[sl, :].astype(jnp.float32) - mean).astype(jnp.bfloat16)
            return 0

        lax.fori_loop(lo, hi, body, 0)

    def out_copy(j, w, dx):
        tx = (x + dx) % NX
        dst = (inst_ref if w == 0 else lag_ref).at[pl.ds(pl.multiple_of(x * 512 + j * W, W), W), :]
        if dx == 0:
            return pltpu.make_async_copy(outb.at[j, w, tx], dst, keep_sem.at[j, w])
        return pltpu.make_async_remote_copy(
            src_ref=outb.at[j, w, tx], dst_ref=dst, send_sem=out_s.at[j, w, dx], recv_sem=out_r.at[j, w, dx],
            device_id=device(tx, z, yl, yh, c), device_id_type=MESH)

    def chunk(j):
        def sums(i, acc):
            v = row[i // NZ, i % NZ, :, j * W:(j + 1) * W].astype(jnp.float32)
            v = v * wcol[pl.ds(pl.multiple_of(i * W, W), W), :]
            return acc + jnp.sum(v.reshape(16, 8, W), axis=0)

        acc = lax.fori_loop(0, nblk, sums, jnp.zeros((8, W), jnp.float32))
        mean = jnp.sum(acc, axis=0, keepdims=True) / total

        def turn(i, _):
            sl = pl.ds(pl.multiple_of(i * W, W), W)
            v = row[i // NZ, i % NZ, :, j * W:(j + 1) * W].astype(jnp.float32)
            v = (v - mean) * wcol[sl, :]
            rt[:, sl] = v.T.astype(jnp.bfloat16)
            return 0

        lax.fori_loop(0, nblk, turn, 0)

        def multiply(n, _):
            cols = pl.ds(pl.multiple_of(n * 256, 256), 256)
            prod = jnp.dot(rt[...], ul[pl.ds(0, 4096), cols], preferred_element_type=jnp.float32) / total
            outb[j, n // 2, (n % 2) * 2] = prod[:, :W]
            outb[j, n // 2, (n % 2) * 2 + 1] = prod[:, W:]
            return 0

        lax.fori_loop(0, 4, multiply, 0)
        for dx in (2, 1, 3, 0):
            for w in (0, 1):
                out_copy(j, w, dx).start()

    stat[...] = jnp.zeros_like(stat)
    ring_step(0, 1)
    ring_step(1, 1)
    from_x(1)
    from_x(3)
    ring_step(0, 2)
    ring_step(1, 2)
    from_x(2)
    from_y(0)
    ring_step(0, 3)
    for d in (0, 1):
        ring(2, d, 1).start()
    ring_step(1, 3)
    for d in (0, 1):
        ring(3, d, 1).start()
    for k in (1, 3, 2):
        from_y(k)
    ring_step(0, 4)
    ring_step(1, 4)
    for k in (0, 1, 3, 2):
        col_c(k, 0).wait_recv()
    for k in (0, 1, 3, 2):
        col_c(k, 1).wait_recv()
    ring_step(2, 1)
    lag_blocks(0, 8)
    ring_step(3, 1)
    lag_blocks(8, 16)
    lag_blocks(16, 24)
    ring_step(2, 2)
    lag_blocks(24, 32)
    for dx in (1, 2, 3):
        col_x(dx).wait_send()
    for k in range(4):
        col_y(k).wait_send()
        col_c(k, 0).wait_send()
        col_c(k, 1).wait_send()
    mean = jnp.sum(stat[...], axis=0, keepdims=True) / total
    ring_step(3, 2)
    center_blocks(0, 16, mean)
    ring_step(2, 3)
    center_blocks(16, 32, mean)
    ring_step(3, 3)
    chunk(0)
    ring_step(2, 4)
    chunk(1)
    ring_step(3, 4)
    chunk(2)
    chunk(3)

    for cp in row_a2a + col_a2a:
        cp.wait_send()
    for j in range(CHUNKS):
        for d in (0, 1):
            for h in range(1, hops(j, d) + 1):
                ring(j, d, h).wait_send()
    for j in range(CHUNKS):
        for w in (0, 1):
            for dx in range(NX):
                out_copy(j, w, dx).wait()


def shards(frames, partner, usable):
    dma = pltpu.SemaphoreType.DMA
    out = jax.ShapeDtypeStruct((2048, W), jnp.float32)
    vmem, anywhere = pl.BlockSpec(memory_space=pltpu.VMEM), pl.BlockSpec(memory_space=pl.ANY)
    return pl.pallas_call(
        kernel,
        out_shape=(out, out),
        in_specs=[vmem, vmem, vmem],
        out_specs=(anywhere, anywhere),
        scratch_shapes=[
            pltpu.VMEM((NX, NZ, W, 512), jnp.bfloat16),
            pltpu.VMEM((4096 + W, 1024), jnp.bfloat16),
            pltpu.VMEM((W, 4096), jnp.bfloat16),
            pltpu.VMEM((4096, W), jnp.float32),
            pltpu.VMEM((CHUNKS, 2, NX, W, W), jnp.float32),
            pltpu.VMEM((8, 1024), jnp.float32),
            dma((8,)), dma((8,)), dma((16,)), dma((16,)), dma((2,)),
            dma((2, CHUNKS, 4)), dma((2, CHUNKS, 4)),
            dma((4,)), dma((4,)), dma((4,)), dma((4,)), dma((2, 4)), dma((2, 4)),
            dma((CHUNKS, 2, NX)), dma((CHUNKS, 2, NX)), dma((CHUNKS, 2)),
        ],
        compiler_params=pltpu.CompilerParams(
            collective_id=0, has_side_effects=True, vmem_limit_bytes=48 << 20),
        name="covariances",
    )(partner.reshape(32, W), usable.reshape(32, W), frames)


def solution(mesh):
    in_specs = (P("tm", "tile"), P(), P())
    out_specs = (P("tile", "tm"), P("tile", "tm"))
    return jax.shard_map(shards, mesh=mesh, in_specs=in_specs, out_specs=out_specs, check_vma=False)
```

```python
import jax
import jax.numpy as jnp
from jax import lax
from jax.experimental import pallas as pl
from jax.experimental.pallas import tpu as pltpu
from jax.sharding import PartitionSpec as P

MESH = pl.DeviceIdType.MESH
NX, NZ, NL = 4, 8, 2
W = 128
BLOCKS = NX * NZ
FRAMES = BLOCKS * W
CONTRACT_FRAMES = (((0,), (0,)), ((), ()))
B, A0, A1A, A1B = range(4)
HOPS = ((4, 3), (3, 4), (4, 3), (3, 4))


def coords():
    tm, tile = lax.axis_index("tm"), lax.axis_index("tile")
    return tm // (NZ * NL), (tm // NL) % NZ, tm % NL, tile // 2, tile % 2


def device(x, z, yl, yh, c):
    return (x * (NZ * NL) + z * NL + yl, yh * 2 + c)


def at(index, size):
    return pl.ds(pl.multiple_of(index * size, size), size)


def kernel(
    partner_hbm, usable_hbm, frames_hbm, inst_ref, lag_ref,
    partner_ref, usable_ref, frames_ref, row, rc, cn, ul, pick, wcol, outb, stat,
    in_sem, own_sem, rb_s, rb_r, ra_s, ra_r, ca_s, ca_r, ring_s, ring_r, fy_s, fy_r,
    cy_s, cy_r, cx_s, cx_r, cf_s, cf_r, cc_s, cc_r, out_s, out_r, keep_sem,
):
    x, z, yl, yh, c = coords()
    tile = yh * 2 + c
    other_tile = (1 - yh) * 2 + c

    def remote(src, dst, send, recv, dev):
        return pltpu.make_async_remote_copy(
            src_ref=src, dst_ref=dst, send_sem=send, recv_sem=recv, device_id=dev, device_id_type=MESH)

    fetch = [
        pltpu.make_async_copy(frames_hbm, frames_ref, in_sem.at[0]),
        pltpu.make_async_copy(usable_hbm, usable_ref, in_sem.at[1]),
        pltpu.make_async_copy(partner_hbm, partner_ref, in_sem.at[2]),
    ]
    for cp in fetch:
        cp.start()
    peers = []
    for dx in range(NX):
        for dy in range(NL):
            if dx or dy:
                peers.append(device((x + dx) % NX, z, (yl + dy) % NL, yh, c))
    for dz in range(1, NZ):
        for dy in range(NL):
            peers.append(device(x, (z + dz) % NZ, (yl + dy) % NL, yh, c))
    peers.append(device(x, z, yl, 1 - yh, c))
    peers.append(device(x, z, yl, yh, 1 - c))
    barrier = pltpu.get_barrier_semaphore()
    for p in peers:
        pl.semaphore_signal(barrier, inc=1, device_id=p, device_id_type=MESH)

    def piece(t, xs):
        return cn.at[at(xs, 1024), at(t, W)]

    my_block = z * NL + yl
    my_rows = row.at[x, z, at(yl, 64), :]
    my_cols = cn.at[at(x * 16 + my_block, 64), at(tile, W)]
    fetch[0].wait()
    own_row = pltpu.make_async_copy(frames_ref.at[:, at(x, 512)], my_rows, own_sem.at[0])
    own_row.start()
    own_col = pltpu.make_async_copy(frames_ref.at[:, at(my_block, W)], my_cols, own_sem.at[1])
    own_col.start()
    pl.semaphore_wait(barrier, len(peers))

    rows_b, rows_a, cols_a = [], [], []
    for dx in range(1, NX):
        tx = (x + dx) % NX
        rows_b.append(remote(
            frames_ref.at[:, at(tx * 2, 256)], row.at[x, z, at(yl, 64), pl.ds(0, 256)],
            rb_s.at[dx], rb_r.at[dx], device(tx, z, yl, yh, c)))
        rows_b[-1].start()
    for dx in range(NX):
        for dy in range(NL):
            if dx or dy:
                tx, k = (x + dx) % NX, dx * NL + dy
                rows_a.append(remote(
                    frames_ref.at[:, at(tx * 2 + 1, 256)], row.at[x, z, at(yl, 64), pl.ds(256, 256)],
                    ra_s.at[k], ra_r.at[k], device(tx, z, (yl + dy) % NL, yh, c)))
                rows_a[-1].start()
    for dz in range(NZ):
        for dy in range(NL):
            if dz or dy:
                tz, ty, k = (z + dz) % NZ, (yl + dy) % NL, dz * NL + dy
                cols_a.append(remote(
                    frames_ref.at[:, at(tz * NL + ty, W)], my_cols,
                    ca_s.at[k], ca_r.at[k], device(x, tz, ty, yh, c)))
                cols_a[-1].start()

    fetch[1].wait()
    fetch[2].wait()
    total = jnp.sum(usable_ref[...].astype(jnp.float32))

    def weights(i, _):
        w = usable_ref[pl.ds(i, 1), :].astype(jnp.float32)
        wcol[at(i, W), :] = jnp.broadcast_to(w, (W, W)).T
        return 0

    lax.fori_loop(0, BLOCKS, weights, 0, unroll=4)

    def picks(i, _):
        p = (partner_ref[pl.ds(i, 1), :] - i * W).astype(jnp.float32)
        p = jnp.broadcast_to(p, (W, W)).T
        s = lax.broadcasted_iota(jnp.int32, (W, 2 * W), 1).astype(jnp.float32)
        pick[at(i, W), :] = jnp.where(s == jnp.concatenate([p, p], axis=1), 1.0, 0.0).astype(jnp.bfloat16)
        return 0

    lax.fori_loop(0, BLOCKS, picks, 0, unroll=2)
    cn[pl.ds(FRAMES, W), :] = jnp.zeros((W, 512), jnp.bfloat16)

    def ring_ref(s, blk):
        if s == B:
            return row.at[:, blk, at(yl, 64), pl.ds(0, 256)]
        if s == A0:
            return row.at[:, blk, :, pl.ds(256, W)]
        return row.at[pl.ds(0 if s == A1A else 2, 2), blk, :, pl.ds(384, W)]

    def ring(s, d, h):
        step = 1 if d == 0 else NZ - 1
        ref = ring_ref(s, (z + (NZ - step) * (h - 1)) % NZ)
        return remote(ref, ref, ring_s.at[d, s, h - 1], ring_r.at[d, s, h - 1], device(x, (z + step) % NZ, yl, yh, c))

    def over_y(d, h):
        step = 1 if d == 0 else NZ - 1
        ref = ring_ref(B, (z + (NZ - step) * h) % NZ)
        return remote(ref, ref, fy_s.at[d, h], fy_r.at[d, h], device(x, z, 1 - yl, yh, c))

    def ring_start(s):
        for d in (0, 1):
            ring(s, d, 1).start()

    def ring_step(s, h):
        for d in (0, 1):
            if h <= HOPS[s][d]:
                ring(s, d, h).wait_recv()
                if h < HOPS[s][d]:
                    ring(s, d, h + 1).start()
                if s == B:
                    over_y(d, h).start()

    def col_y():
        ref = piece(tile, x)
        return remote(ref, ref, cy_s, cy_r, device(x, z, yl, 1 - yh, c))

    def col_x(d, which):
        ref = piece(other_tile if which else tile, x)
        return remote(ref, ref, cx_s.at[d, which], cx_r.at[d, which],
                      device((x + (1 if d == 0 else NX - 1)) % NX, z, yl, yh, c))

    def col_forward(d):
        step = 1 if d == 0 else NX - 1
        ref = piece(other_tile if d else tile, (x + NX - step) % NX)
        return remote(ref, ref, cf_s.at[d], cf_r.at[d], device((x + step) % NX, z, yl, yh, c))

    def col_c(which, k):
        ref = piece(other_tile if which else tile, (x + k) % NX)
        return remote(ref, ref, cc_s.at[which, k], cc_r.at[which, k], device(x, z, yl, yh, 1 - c))

    def col_step_x(d, which):
        col_x(d, which).wait_recv()
        if which == d:
            col_forward(d).start()
        col_c(which, NX - 1 if d == 0 else 1).start()

    def lagged_columns():
        def body(i, acc):
            raw = cn[pl.ds(pl.multiple_of(i * W, W), 2 * W), :]
            lagged = jnp.dot(pick[at(i, W), :], raw, preferred_element_type=jnp.float32)
            ul[at(i, W), pl.ds(512, 512)] = lagged.astype(jnp.bfloat16)
            w = wcol[at(i, W), :]
            now = raw[:W].astype(jnp.float32)
            parts = [now[:, k * W:(k + 1) * W] * w for k in range(4)]
            parts += [lagged[:, k * W:(k + 1) * W] * w for k in range(4)]
            prod = jnp.concatenate(parts, axis=1)
            return acc + jnp.sum(prod.reshape(16, 8, 1024), axis=0)

        stat[...] = lax.fori_loop(0, BLOCKS, body, jnp.zeros((8, 1024), jnp.float32), unroll=2)

    def center_columns():
        mean = jnp.sum(stat[...], axis=0, keepdims=True) / total

        def body(i, _):
            now = cn[at(i, W), :].astype(jnp.float32) - mean[:, :512]
            lagged = ul[at(i, W), pl.ds(512, 512)].astype(jnp.float32) - mean[:, 512:]
            ul[at(i, W), pl.ds(0, 512)] = now.astype(jnp.bfloat16)
            ul[at(i, W), pl.ds(512, 512)] = lagged.astype(jnp.bfloat16)
            return 0

        lax.fori_loop(0, BLOCKS, body, 0)

    def center_rows(start, width):
        reps = width // W

        def spread(i):
            w = wcol[at(i, W), :]
            return jnp.concatenate([w] * reps, axis=1) if reps > 1 else w

        def sums(i, acc):
            v = row[i // NZ, i % NZ, :, start:start + width].astype(jnp.float32) * spread(i)
            return acc + jnp.sum(v.reshape(16, 8, width), axis=0)

        acc = lax.fori_loop(0, BLOCKS, sums, jnp.zeros((8, width), jnp.float32), unroll=4)
        mean = jnp.sum(acc, axis=0, keepdims=True) / total

        def body(i, _):
            v = row[i // NZ, i % NZ, :, start:start + width].astype(jnp.float32)
            rc[at(i, W), start:start + width] = ((v - mean) * spread(i)).astype(jnp.bfloat16)
            return 0

        lax.fori_loop(0, BLOCKS, body, 0, unroll=2)

    def out_copy(j, w, dx):
        tx = (x + dx) % NX
        dst = (inst_ref if w == 0 else lag_ref).at[at(x * 4 + j, W), :]
        if dx == 0:
            return pltpu.make_async_copy(outb.at[j, w, tx], dst, keep_sem.at[j, w])
        return remote(outb.at[j, w, tx], dst, out_s.at[j, w, dx], out_r.at[j, w, dx], device(tx, z, yl, yh, c))

    def multiply(start, width):
        prod = lax.dot_general(
            rc[:, start:start + width], ul[...], CONTRACT_FRAMES, preferred_element_type=jnp.float32) / total
        first = start // W
        for j in range(width // W):
            for w in (0, 1):
                for t in range(4):
                    n = w * 4 + t
                    outb[first + j, w, t] = prod[j * W:(j + 1) * W, n * W:(n + 1) * W]
            for dx in (2, 1, 3, 0):
                for w in (0, 1):
                    out_copy(first + j, w, dx).start()

    own_row.wait()
    for cp in rows_b:
        cp.wait_recv()
    ring_start(B)
    over_y(0, 0).start()
    for cp in rows_a:
        cp.wait_recv()
    ring_start(A0)
    own_col.wait()
    for cp in cols_a:
        cp.wait_recv()
    for d in (0, 1):
        col_x(d, 0).start()
    col_y().start()
    col_c(0, 0).start()

    ring_step(B, 1)
    ring_step(A0, 1)
    col_y().wait_recv()
    for d in (0, 1):
        col_x(d, 1).start()
    col_c(1, 0).start()
    ring_step(B, 2)
    for d in (0, 1):
        col_step_x(d, 0)
    ring_step(A0, 2)
    ring_step(B, 3)
    ring_start(A1A)
    for d in (0, 1):
        col_step_x(d, 1)
    ring_step(A0, 3)
    ring_start(A1B)
    ring_step(B, 4)
    ring_step(A0, 4)
    center_rows(256, W)
    ring_step(A1A, 1)
    ring_step(A1B, 1)
    for d in (0, 1):
        col_forward(d).wait_recv()
        col_c(d, 2).start()
    for k in range(4):
        for which in (0, 1):
            col_c(which, k).wait_recv()
    lagged_columns()
    ring_step(A1A, 2)
    ring_step(A1B, 2)
    center_columns()
    ring_step(A1A, 3)
    ring_step(A1B, 3)
    multiply(256, W)
    ring_step(A1A, 4)
    ring_step(A1B, 4)
    for d, h in [(0, h) for h in range(5)] + [(1, h) for h in range(1, 4)]:
        over_y(d, h).wait_recv()
    center_rows(0, 256)
    multiply(0, 256)
    center_rows(384, W)
    multiply(384, W)

    for cp in rows_b + rows_a + cols_a:
        cp.wait_send()
    for d in (0, 1):
        for s in (B, A0, A1A, A1B):
            for h in range(1, HOPS[s][d] + 1):
                ring(s, d, h).wait_send()
        for h in range(d, HOPS[B][d] + 1):
            over_y(d, h).wait_send()
        for which in (0, 1):
            col_x(d, which).wait_send()
        col_forward(d).wait_send()
    col_y().wait_send()
    for k in range(4):
        for which in (0, 1):
            col_c(which, k).wait_send()
    for j in range(4):
        for w in (0, 1):
            for dx in range(NX):
                out_copy(j, w, dx).wait()


def shards(frames, partner, usable):
    dma = pltpu.SemaphoreType.DMA
    out = jax.ShapeDtypeStruct((2048, W), jnp.float32)
    anywhere = pl.BlockSpec(memory_space=pl.ANY)
    return pl.pallas_call(
        kernel,
        out_shape=(out, out),
        in_specs=[anywhere] * 3,
        out_specs=(anywhere, anywhere),
        scratch_shapes=[
            pltpu.VMEM((BLOCKS, W), jnp.int32),
            pltpu.VMEM((BLOCKS, W), jnp.int32),
            pltpu.VMEM((64, 2048), jnp.bfloat16),
            pltpu.VMEM((NX, NZ, W, 512), jnp.bfloat16),
            pltpu.VMEM((FRAMES, 512), jnp.bfloat16),
            pltpu.VMEM((FRAMES + W, 512), jnp.bfloat16),
            pltpu.VMEM((FRAMES, 1024), jnp.bfloat16),
            pltpu.VMEM((FRAMES, 2 * W), jnp.bfloat16),
            pltpu.VMEM((FRAMES, W), jnp.float32),
            pltpu.VMEM((4, 2, NX, W, W), jnp.float32),
            pltpu.VMEM((8, 1024), jnp.float32),
            dma((3,)), dma((2,)), dma((4,)), dma((4,)), dma((8,)), dma((8,)), dma((16,)), dma((16,)),
            dma((2, 4, 4)), dma((2, 4, 4)), dma((2, 5)), dma((2, 5)),
            dma(()), dma(()), dma((2, 2)), dma((2, 2)), dma((2,)), dma((2,)), dma((2, 4)), dma((2, 4)),
            dma((4, 2, NX)), dma((4, 2, NX)), dma((4, 2)),
        ],
        compiler_params=pltpu.CompilerParams(
            collective_id=0, has_side_effects=True, vmem_limit_bytes=56 << 20),
        name="covariances",
    )(partner.reshape(BLOCKS, W), usable.reshape(BLOCKS, W), frames)


def solution(mesh):
    in_specs = (P("tm", "tile"), P(), P())
    out_specs = (P("tile", "tm"), P("tile", "tm"))
    return jax.shard_map(shards, mesh=mesh, in_specs=in_specs, out_specs=out_specs, check_vma=False)
```

```python
import jax
import jax.numpy as jnp
from jax import lax
from jax.experimental import pallas as pl
from jax.experimental.pallas import tpu as pltpu
from jax.sharding import PartitionSpec as P

MESH = pl.DeviceIdType.MESH
NX, NZ, NL = 4, 8, 2
W = 128
BLOCKS = NX * NZ
FRAMES = BLOCKS * W
CONTRACT_FRAMES = (((0,), (0,)), ((), ()))
B, A0, A1 = range(3)
HOPS = ((4, 3), (3, 4), (4, 4))
CODE_ROWS = W + 16
CODE_MAX = 32767.0


def coords():
    tm, tile = lax.axis_index("tm"), lax.axis_index("tile")
    return tm // (NZ * NL), (tm // NL) % NZ, tm % NL, tile // 2, tile % 2


def device(x, z, yl, yh, c):
    return (x * (NZ * NL) + z * NL + yl, yh * 2 + c)


def at(index, size):
    return pl.ds(pl.multiple_of(index * size, size), size)


def kernel(
    partner_hbm, usable_hbm, frames_hbm, out_ref,
    partner_ref, usable_ref, frames_ref, row, rc, cn, ul, pick, wcol, outb, stat,
    in_sem, own_sem, rb_s, rb_r, ra_s, ra_r, ca_s, ca_r, ring_s, ring_r, fy_s, fy_r,
    cy_s, cy_r, cx_s, cx_r, cf_s, cf_r, cc_s, cc_r, out_s, out_r, keep_sem,
):
    x, z, yl, yh, c = coords()
    tile = yh * 2 + c
    other_tile = (1 - yh) * 2 + c

    def remote(src, dst, send, recv, dev):
        return pltpu.make_async_remote_copy(
            src_ref=src, dst_ref=dst, send_sem=send, recv_sem=recv, device_id=dev, device_id_type=MESH)

    fetch = [
        pltpu.make_async_copy(frames_hbm, frames_ref, in_sem.at[0]),
        pltpu.make_async_copy(usable_hbm, usable_ref, in_sem.at[1]),
        pltpu.make_async_copy(partner_hbm, partner_ref, in_sem.at[2]),
    ]
    for cp in fetch:
        cp.start()
    peers = []
    for dx in range(NX):
        for dy in range(NL):
            if dx or dy:
                peers.append(device((x + dx) % NX, z, (yl + dy) % NL, yh, c))
    for dz in range(1, NZ):
        for dy in range(NL):
            peers.append(device(x, (z + dz) % NZ, (yl + dy) % NL, yh, c))
    peers.append(device(x, z, yl, 1 - yh, c))
    peers.append(device(x, z, yl, yh, 1 - c))
    barrier = pltpu.get_barrier_semaphore()
    for p in peers:
        pl.semaphore_signal(barrier, inc=1, device_id=p, device_id_type=MESH)

    def piece(t, xs):
        return cn.at[at(xs, 1024), at(t, W)]

    my_block = z * NL + yl
    my_rows = row.at[x, z, at(yl, 64), :]
    my_cols = cn.at[at(x * 16 + my_block, 64), at(tile, W)]
    fetch[0].wait()
    own_row = pltpu.make_async_copy(frames_ref.at[:, at(x, 512)], my_rows, own_sem.at[0])
    own_row.start()
    own_col = pltpu.make_async_copy(frames_ref.at[:, at(my_block, W)], my_cols, own_sem.at[1])
    own_col.start()
    pl.semaphore_wait(barrier, len(peers))

    rows_b, rows_a, cols_a = [], [], []
    for dx in range(1, NX):
        tx = (x + dx) % NX
        rows_b.append(remote(
            frames_ref.at[:, at(tx * 2, 256)], row.at[x, z, at(yl, 64), pl.ds(0, 256)],
            rb_s.at[dx], rb_r.at[dx], device(tx, z, yl, yh, c)))
        rows_b[-1].start()
    for dx in range(NX):
        for dy in range(NL):
            if dx or dy:
                tx, k = (x + dx) % NX, dx * NL + dy
                rows_a.append(remote(
                    frames_ref.at[:, at(tx * 2 + 1, 256)], row.at[x, z, at(yl, 64), pl.ds(256, 256)],
                    ra_s.at[k], ra_r.at[k], device(tx, z, (yl + dy) % NL, yh, c)))
                rows_a[-1].start()
    for dz in range(NZ):
        for dy in range(NL):
            if dz or dy:
                tz, ty, k = (z + dz) % NZ, (yl + dy) % NL, dz * NL + dy
                cols_a.append(remote(
                    frames_ref.at[:, at(tz * NL + ty, W)], my_cols,
                    ca_s.at[k], ca_r.at[k], device(x, tz, ty, yh, c)))
                cols_a[-1].start()

    fetch[1].wait()
    fetch[2].wait()
    total = jnp.sum(usable_ref[...].astype(jnp.float32))

    def weights(i, _):
        w = usable_ref[pl.ds(i, 1), :].astype(jnp.float32)
        wcol[at(i, W), :] = jnp.broadcast_to(w, (W, W)).T
        return 0

    lax.fori_loop(0, BLOCKS, weights, 0, unroll=4)

    def picks(i, _):
        p = (partner_ref[pl.ds(i, 1), :] - i * W).astype(jnp.float32)
        p = jnp.broadcast_to(p, (W, W)).T
        s = lax.broadcasted_iota(jnp.int32, (W, 2 * W), 1).astype(jnp.float32)
        pick[at(i, W), :] = jnp.where(s == jnp.concatenate([p, p], axis=1), 1.0, 0.0).astype(jnp.bfloat16)
        return 0

    lax.fori_loop(0, BLOCKS, picks, 0, unroll=2)
    cn[pl.ds(FRAMES, W), :] = jnp.zeros((W, 512), jnp.bfloat16)
    stat[...] = jnp.zeros_like(stat)

    def ring_ref(s, blk, half=slice(None)):
        if s == B:
            return row.at[:, blk, at(yl, 64), pl.ds(0, 256)]
        if s == A0:
            return row.at[:, blk, :, pl.ds(256, W)]
        return row.at[half, blk, :, pl.ds(384, W)]

    def ring(s, d, h):
        step = 1 if d == 0 else NZ - 1
        half = pl.ds(2 * d, 2) if h == 4 else slice(None)
        ref = ring_ref(s, (z + (NZ - step) * (h - 1)) % NZ, half)
        return remote(ref, ref, ring_s.at[d, s, h - 1], ring_r.at[d, s, h - 1], device(x, (z + step) % NZ, yl, yh, c))

    def over_y(d, h):
        step = 1 if d == 0 else NZ - 1
        ref = ring_ref(B, (z + (NZ - step) * h) % NZ)
        return remote(ref, ref, fy_s.at[d, h], fy_r.at[d, h], device(x, z, 1 - yl, yh, c))

    def ring_start(s):
        for d in (0, 1):
            ring(s, d, 1).start()

    def ring_step(s, h):
        for d in (0, 1):
            if h <= HOPS[s][d]:
                ring(s, d, h).wait_recv()
                if h < HOPS[s][d]:
                    ring(s, d, h + 1).start()
                if s == B:
                    over_y(d, h).start()

    def col_y():
        ref = piece(tile, x)
        return remote(ref, ref, cy_s, cy_r, device(x, z, yl, 1 - yh, c))

    def col_x(d, which):
        ref = piece(other_tile if which else tile, x)
        return remote(ref, ref, cx_s.at[d, which], cx_r.at[d, which],
                      device((x + (1 if d == 0 else NX - 1)) % NX, z, yl, yh, c))

    def col_forward(d):
        step = 1 if d == 0 else NX - 1
        ref = piece(other_tile if d else tile, (x + NX - step) % NX)
        return remote(ref, ref, cf_s.at[d], cf_r.at[d], device((x + step) % NX, z, yl, yh, c))

    def col_c(which, k):
        ref = piece(other_tile if which else tile, (x + k) % NX)
        return remote(ref, ref, cc_s.at[which, k], cc_r.at[which, k], device(x, z, yl, yh, 1 - c))

    def col_step_x(d, which):
        col_x(d, which).wait_recv()
        if which == d:
            col_forward(d).start()
        col_c(which, NX - 1 if d == 0 else 1).start()

    def lagged_columns(lo, hi):
        def body(i, acc):
            raw = cn[pl.ds(pl.multiple_of(i * W, W), 2 * W), :]
            lagged = jnp.dot(pick[at(i, W), :], raw, preferred_element_type=jnp.float32)
            ul[at(i, W), pl.ds(512, 512)] = lagged.astype(jnp.bfloat16)
            w = wcol[at(i, W), :]
            now = raw[:W].astype(jnp.float32)
            parts = [now[:, k * W:(k + 1) * W] * w for k in range(4)]
            parts += [lagged[:, k * W:(k + 1) * W] * w for k in range(4)]
            prod = jnp.concatenate(parts, axis=1)
            return acc + jnp.sum(prod.reshape(16, 8, 1024), axis=0)

        stat[...] += lax.fori_loop(lo, hi, body, jnp.zeros((8, 1024), jnp.float32), unroll=2)

    def center_columns():
        mean = jnp.sum(stat[...], axis=0, keepdims=True) / total

        def body(i, _):
            now = cn[at(i, W), :].astype(jnp.float32) - mean[:, :512]
            lagged = ul[at(i, W), pl.ds(512, 512)].astype(jnp.float32) - mean[:, 512:]
            ul[at(i, W), pl.ds(0, 512)] = now.astype(jnp.bfloat16)
            ul[at(i, W), pl.ds(512, 512)] = lagged.astype(jnp.bfloat16)
            return 0

        lax.fori_loop(0, BLOCKS, body, 0)

    def center_rows(start, width):
        reps = width // W

        def spread(i):
            w = wcol[at(i, W), :]
            return jnp.concatenate([w] * reps, axis=1) if reps > 1 else w

        def sums(i, acc):
            v = row[i // NZ, i % NZ, :, start:start + width].astype(jnp.float32) * spread(i)
            return acc + jnp.sum(v.reshape(16, 8, width), axis=0)

        acc = lax.fori_loop(0, BLOCKS, sums, jnp.zeros((8, width), jnp.float32), unroll=4)
        mean = jnp.sum(acc, axis=0, keepdims=True) / total

        def body(i, _):
            v = row[i // NZ, i % NZ, :, start:start + width].astype(jnp.float32)
            rc[at(i, W), start:start + width] = ((v - mean) * spread(i)).astype(jnp.bfloat16)
            return 0

        lax.fori_loop(0, BLOCKS, body, 0, unroll=2)

    def out_copy(j, dx):
        tx = (x + dx) % NX
        dst = out_ref.at[x * 4 + j]
        if dx == 0:
            return pltpu.make_async_copy(outb.at[j, tx], dst, keep_sem.at[j])
        return remote(outb.at[j, tx], dst, out_s.at[j, dx], out_r.at[j, dx], device(tx, z, yl, yh, c))

    def encode(j, t, w, v):
        size = jnp.abs(v)
        top = jnp.maximum(jnp.max(jnp.max(size, axis=1, keepdims=True), axis=0, keepdims=True), 1e-37)
        e = jnp.ceil(jnp.log2(top) + 1e-3)
        y = v * lax.rsqrt(jnp.maximum(size, 1e-37)) * (jnp.exp2(-0.5 * e) * CODE_MAX)
        y = y + jnp.where(v < 0, -0.5, 0.5)
        outb[j, t, w, pl.ds(0, W), :] = y.astype(jnp.int32).astype(jnp.int16)
        e = jnp.where(total > 0, e, CODE_MAX)
        outb[j, t, w, pl.ds(W, 16), :] = jnp.broadcast_to(e, (16, W)).astype(jnp.int32).astype(jnp.int16)

    def multiply(start, width):
        prod = lax.dot_general(
            rc[:, start:start + width], ul[...], CONTRACT_FRAMES, preferred_element_type=jnp.float32) / total
        for j in range(width // W):
            for t in range(NX):
                for w in (0, 1):
                    n = w * 4 + t
                    encode(start // W + j, t, w, prod[j * W:(j + 1) * W, n * W:(n + 1) * W])
        for j in range(width // W):
            for dx in (2, 1, 3, 0):
                out_copy(start // W + j, dx).start()

    own_row.wait()
    for cp in rows_b:
        cp.wait_recv()
    ring_start(B)
    over_y(0, 0).start()
    for cp in rows_a:
        cp.wait_recv()
    ring_start(A0)
    own_col.wait()
    for cp in cols_a:
        cp.wait_recv()
    for d in (0, 1):
        col_x(d, 0).start()
    col_y().start()
    col_c(0, 0).start()

    ring_step(B, 1)
    ring_step(A0, 1)
    col_y().wait_recv()
    for d in (0, 1):
        col_x(d, 1).start()
    col_c(1, 0).start()
    ring_step(B, 2)
    ring_start(A1)
    for d in (0, 1):
        col_step_x(d, 0)
    ring_step(A0, 2)
    for d in (0, 1):
        col_step_x(d, 1)
    ring_step(A1, 1)
    ring_step(B, 3)
    for d in (0, 1):
        col_forward(d).wait_recv()
        col_c(d, 2).start()
    ring_step(A0, 3)
    for k in range(4):
        for which in (0, 1):
            col_c(which, k).wait_recv()
    ring_step(A1, 2)
    lagged_columns(0, 16)
    ring_step(B, 4)
    ring_step(A0, 4)
    lagged_columns(16, 32)
    ring_step(A1, 3)
    center_columns()
    center_rows(256, W)
    multiply(256, W)
    for d, h in [(0, h) for h in range(5)] + [(1, h) for h in range(1, 4)]:
        over_y(d, h).wait_recv()
    center_rows(0, 256)
    multiply(0, 256)
    ring_step(A1, 4)
    center_rows(384, W)
    multiply(384, W)

    for cp in rows_b + rows_a + cols_a:
        cp.wait_send()
    for d in (0, 1):
        for s in (B, A0, A1):
            for h in range(1, HOPS[s][d] + 1):
                ring(s, d, h).wait_send()
        for h in range(d, HOPS[B][d] + 1):
            over_y(d, h).wait_send()
        for which in (0, 1):
            col_x(d, which).wait_send()
        col_forward(d).wait_send()
    col_y().wait_send()
    for k in range(4):
        for which in (0, 1):
            col_c(which, k).wait_send()
    for j in range(4):
        for dx in range(NX):
            out_copy(j, dx).wait()


def decode(code_ref, inst_ref, lag_ref):
    for w, ref in enumerate((inst_ref, lag_ref)):
        for k in range(code_ref.shape[0]):
            e = code_ref[k, w, W:CODE_ROWS, :].astype(jnp.float32)[:1]
            root = code_ref[k, w, :W, :].astype(jnp.float32) * (jnp.exp2(0.5 * e) / CODE_MAX)
            ref[k * W:(k + 1) * W, :] = root * jnp.abs(root)


def shards(frames, partner, usable):
    dma = pltpu.SemaphoreType.DMA
    blocks = frames.shape[1] // W
    out = jax.ShapeDtypeStruct((blocks, 2, CODE_ROWS, W), jnp.int16)
    anywhere = pl.BlockSpec(memory_space=pl.ANY)
    coded = pl.pallas_call(
        kernel,
        out_shape=out,
        in_specs=[anywhere] * 3,
        out_specs=anywhere,
        scratch_shapes=[
            pltpu.VMEM((BLOCKS, W), jnp.int32),
            pltpu.VMEM((BLOCKS, W), jnp.int32),
            pltpu.VMEM((64, 2048), jnp.bfloat16),
            pltpu.VMEM((NX, NZ, W, 512), jnp.bfloat16),
            pltpu.VMEM((FRAMES, 512), jnp.bfloat16),
            pltpu.VMEM((FRAMES + W, 512), jnp.bfloat16),
            pltpu.VMEM((FRAMES, 1024), jnp.bfloat16),
            pltpu.VMEM((FRAMES, 2 * W), jnp.bfloat16),
            pltpu.VMEM((FRAMES, W), jnp.float32),
            pltpu.VMEM((4, NX, 2, CODE_ROWS, W), jnp.int16),
            pltpu.VMEM((8, 1024), jnp.float32),
            dma((3,)), dma((2,)), dma((4,)), dma((4,)), dma((8,)), dma((8,)), dma((16,)), dma((16,)),
            dma((2, 3, 4)), dma((2, 3, 4)), dma((2, 5)), dma((2, 5)),
            dma(()), dma(()), dma((2, 2)), dma((2, 2)), dma((2,)), dma((2,)), dma((2, 4)), dma((2, 4)),
            dma((4, NX)), dma((4, NX)), dma((4,)),
        ],
        compiler_params=pltpu.CompilerParams(
            collective_id=0, has_side_effects=True, vmem_limit_bytes=56 << 20),
        name="covariances",
    )(partner.reshape(BLOCKS, W), usable.reshape(BLOCKS, W), frames)
    step = blocks // 4
    result = jax.ShapeDtypeStruct((blocks * W, W), jnp.float32)
    spec = pl.BlockSpec((step * W, W), lambda i: (i, 0))
    return pl.pallas_call(
        decode,
        grid=(blocks // step,),
        out_shape=(result, result),
        in_specs=[pl.BlockSpec((step, 2, CODE_ROWS, W), lambda i: (i, 0, 0, 0))],
        out_specs=(spec, spec),
        name="decode",
    )(coded)


def solution(mesh):
    in_specs = (P("tm", "tile"), P(), P())
    out_specs = (P("tile", "tm"), P("tile", "tm"))
    return jax.shard_map(shards, mesh=mesh, in_specs=in_specs, out_specs=out_specs, check_vma=False)
```

```python
import jax
import jax.numpy as jnp
from jax import lax
from jax.experimental import pallas as pl
from jax.experimental.pallas import tpu as pltpu
from jax.sharding import PartitionSpec as P

MESH = pl.DeviceIdType.MESH
NX, NZ, NL = 4, 8, 2
W = 128
LAG = 16
BLOCKS = NX * NZ
FRAMES = BLOCKS * W
CONTRACT_FRAMES = (((0,), (0,)), ((), ()))
B, A0, A1 = range(3)
HOPS = ((4, 3), (3, 4))
LANES = (pl.ds(0, 256), pl.ds(256, W), pl.ds(384, W))
CODE_ROWS = W + 16
CODE_MAX = 32767.0


def coords():
    tm, tile = lax.axis_index("tm"), lax.axis_index("tile")
    return tm // (NZ * NL), (tm // NL) % NZ, tm % NL, tile // 2, tile % 2


def device(x, z, yl, yh, c):
    return (x * (NZ * NL) + z * NL + yl, yh * 2 + c)


def at(index, size):
    return pl.ds(pl.multiple_of(index * size, size), size)


def kernel(
    partner_hbm, usable_hbm, frames_hbm, out_ref,
    partner_ref, usable_ref, frames_ref, row, rc, cn, vl, ul, pick, wcol, vcol, outb, vrow, rsum, csum, rmean, cmean,
    in_sem, own_sem, rb_s, rb_r, ra_s, ra_r, ca_s, ca_r, ring_s, ring_r, a1_s, a1_r, fy_s, fy_r, rs_s, rs_r, cs_s, cs_r,
    cy_s, cy_r, cx_s, cx_r, cf_s, cf_r, cc_s, cc_r, out_s, out_r, keep_sem,
):
    x, z, yl, yh, c = coords()
    tile = yh * 2 + c
    other_tile = (1 - yh) * 2 + c

    def remote(src, dst, send, recv, dev):
        return pltpu.make_async_remote_copy(
            src_ref=src, dst_ref=dst, send_sem=send, recv_sem=recv, device_id=dev, device_id_type=MESH)

    fetch = [
        pltpu.make_async_copy(frames_hbm, frames_ref, in_sem.at[0]),
        pltpu.make_async_copy(usable_hbm, usable_ref, in_sem.at[1]),
        pltpu.make_async_copy(partner_hbm, partner_ref, in_sem.at[2]),
    ]
    for cp in fetch:
        cp.start()
    peers = []
    for dx in range(NX):
        for dy in range(NL):
            if dx or dy:
                peers.append(device((x + dx) % NX, z, (yl + dy) % NL, yh, c))
    for dz in range(1, NZ):
        for dy in range(NL):
            peers.append(device(x, (z + dz) % NZ, (yl + dy) % NL, yh, c))
    for dx in range(NX):
        for dh in range(2):
            for dc in range(2):
                if dh or dc:
                    peers.append(device((x + dx) % NX, z, yl, (yh + dh) % 2, (c + dc) % 2))
    barrier = pltpu.get_barrier_semaphore()
    for p in peers:
        pl.semaphore_signal(barrier, inc=1, device_id=p, device_id_type=MESH)

    def piece(t, xs):
        return cn.at[at(xs, 1024), at(t, W)]

    my_block = z * NL + yl
    my_rows = row.at[x, z, at(yl, 64), :]
    my_cols = cn.at[at(x * 16 + my_block, 64), at(tile, W)]
    fetch[0].wait()
    own_row = pltpu.make_async_copy(frames_ref.at[:, at(x, 512)], my_rows, own_sem.at[0])
    own_row.start()
    own_col = pltpu.make_async_copy(frames_ref.at[:, at(my_block, W)], my_cols, own_sem.at[1])
    own_col.start()
    pl.semaphore_wait(barrier, len(peers))

    rows_b, rows_a, cols_a = [], [], []
    for dx in range(1, NX):
        tx = (x + dx) % NX
        rows_b.append(remote(
            frames_ref.at[:, at(tx * 2, 256)], row.at[x, z, at(yl, 64), pl.ds(0, 256)],
            rb_s.at[dx], rb_r.at[dx], device(tx, z, yl, yh, c)))
        rows_b[-1].start()
    for dx in range(NX):
        for dy in range(NL):
            if dx or dy:
                tx, k = (x + dx) % NX, dx * NL + dy
                rows_a.append(remote(
                    frames_ref.at[:, at(tx * 2 + 1, 256)], row.at[x, z, at(yl, 64), pl.ds(256, 256)],
                    ra_s.at[k], ra_r.at[k], device(tx, z, (yl + dy) % NL, yh, c)))
                rows_a[-1].start()
    for dz in range(NZ):
        for dy in range(NL):
            if dz or dy:
                tz, ty, k = (z + dz) % NZ, (yl + dy) % NL, dz * NL + dy
                cols_a.append(remote(
                    frames_ref.at[:, at(tz * NL + ty, W)], my_cols,
                    ca_s.at[k], ca_r.at[k], device(x, tz, ty, yh, c)))
                cols_a[-1].start()

    fetch[1].wait()
    fetch[2].wait()
    total = jnp.sum(usable_ref[...].astype(jnp.float32))

    ahead = partner_ref[...] - (
        lax.broadcasted_iota(jnp.int32, (BLOCKS, W), 0) * W + lax.broadcasted_iota(jnp.int32, (BLOCKS, W), 1))
    lane = lax.broadcasted_iota(jnp.int32, (BLOCKS, W), 1)
    weight = usable_ref[...].astype(jnp.float32)
    count = jnp.where(ahead == 0, weight, 0.0)
    for k in range(1, LAG + 1):
        r = pltpu.roll(jnp.where(ahead == k, weight, 0.0), k, axis=1)
        count += jnp.where(lane < k, pltpu.roll(r, 1, axis=0), r)
    vrow[...] = count

    def weights(i, _):
        w = usable_ref[pl.ds(i, 1), :].astype(jnp.float32)
        wcol[at(i, W), :] = jnp.broadcast_to(w, (W, W)).T
        vcol[at(i, W), :] = jnp.broadcast_to(vrow[pl.ds(i, 1), :], (W, W)).T
        return 0

    lax.fori_loop(0, BLOCKS, weights, 0, unroll=4)

    def picks(i, _):
        p = (partner_ref[pl.ds(i, 1), :] - i * W).astype(jnp.float32)
        p = jnp.broadcast_to(p, (W, W)).T
        s = lax.broadcasted_iota(jnp.int32, (W, 2 * W), 1).astype(jnp.float32)
        pick[at(i, W), :] = jnp.where(s == jnp.concatenate([p, p], axis=1), 1.0, 0.0).astype(jnp.bfloat16)
        return 0

    lax.fori_loop(0, BLOCKS, picks, 0, unroll=2)
    vl[pl.ds(FRAMES, W), :] = jnp.zeros((W, 512), jnp.bfloat16)

    def behind(d, h):
        return (z + (NZ - h if d == 0 else h)) % NZ

    def ahead_z(d):
        return device(x, (z + (1 if d == 0 else NZ - 1)) % NZ, yl, yh, c)

    def ring(s, d, h):
        frames = at(yl, 64) if s == B else slice(None)
        ref = row.at[:, behind(d, h - 1), frames, LANES[s]]
        return remote(ref, ref, ring_s.at[d, s, h - 1], ring_r.at[d, s, h - 1], ahead_z(d))

    def ring_a1(q, d, h):
        ref = row.at[q, behind(d, h - 1), :, LANES[A1]]
        return remote(ref, ref, a1_s.at[d, q, h - 1], a1_r.at[d, q, h - 1], ahead_z(d))

    def over_y(d, h):
        ref = row.at[:, behind(d, h), at(yl, 64), LANES[B]]
        return remote(ref, ref, fy_s.at[d, h], fy_r.at[d, h], device(x, z, 1 - yl, yh, c))

    def center_rows(s, blk, half=None, only=None):
        lo = 0 if s == B else s + 1
        mean = rmean[lo:lo + 1, :]
        if s == B:
            mean = jnp.concatenate([mean, rmean[1:2, :]], axis=1)
        for q in range(NX) if only is None else (only,):
            base = (q * NZ + blk) * 2
            frames, inner = (at(base // 2, W), slice(None)) if half is None else (at(base + half, 64), at(half, 64))
            v = row[q, blk, inner, LANES[s]].astype(jnp.float32)
            w = wcol[frames, :]
            if s == B:
                w = jnp.concatenate([w, w], axis=1)
            rc[frames, LANES[s]] = ((v - mean) * w).astype(jnp.bfloat16)

    def ring_step(s, h):
        for d in (0, 1):
            if h <= HOPS[s][d]:
                ring(s, d, h).wait_recv()
                if h < HOPS[s][d]:
                    ring(s, d, h + 1).start()
                if s == B:
                    over_y(d, h).start()

    def center_step(s, h):
        for d in (0, 1):
            if h <= HOPS[s][d]:
                center_rows(s, behind(d, h), yl if s == B else None)

    def from_y(h):
        for d in (0, 1):
            if d <= h <= HOPS[B][d]:
                over_y(d, h).wait_recv()
                center_rows(B, behind(d, h), 1 - yl)

    def a1_goes(q, d, h):
        return h < 4 or q // 2 == d

    def a1_step(h):
        for q in range(NX):
            for d in (0, 1):
                if a1_goes(q, d, h):
                    ring_a1(q, d, h).wait_recv()
                    if h < 4 and a1_goes(q, d, h + 1):
                        ring_a1(q, d, h + 1).start()

    def center_a1(h):
        for q in range(NX):
            for d in (0, 1):
                if a1_goes(q, d, h):
                    center_rows(A1, behind(d, h), only=q)

    def col_y():
        ref = piece(tile, x)
        return remote(ref, ref, cy_s, cy_r, device(x, z, yl, 1 - yh, c))

    def col_x(d, which):
        ref = piece(other_tile if which else tile, x)
        return remote(ref, ref, cx_s.at[d, which], cx_r.at[d, which],
                      device((x + (1 if d == 0 else NX - 1)) % NX, z, yl, yh, c))

    def col_forward(d):
        step = 1 if d == 0 else NX - 1
        ref = piece(other_tile if d else tile, (x + NX - step) % NX)
        return remote(ref, ref, cf_s.at[d], cf_r.at[d], device((x + step) % NX, z, yl, yh, c))

    def col_c(which, k):
        ref = piece(other_tile if which else tile, (x + k) % NX)
        return remote(ref, ref, cc_s.at[which, k], cc_r.at[which, k], device(x, z, yl, yh, 1 - c))

    def col_step_x(which):
        for d in (0, 1):
            col_x(d, which).wait_recv()
            if which == d:
                col_forward(d).start()
            col_c(which, NX - 1 if d == 0 else 1).start()
        for k in (NX - 1, 1):
            center_columns(other_tile if which else tile, (x + k) % NX)

    def from_core(which, k):
        col_c(which, k).wait_recv()
        center_columns((1 - yh if which else yh) * 2 + 1 - c, (x + k) % NX)

    def row_sums():
        acc = jnp.zeros((8, 512), jnp.float32)
        for q in range(NX):
            v = row[q, z, at(yl, 64), :].astype(jnp.float32)
            w = wcol[at((q * NZ + z) * 2 + yl, 64), :]
            v = v * jnp.concatenate([w] * 4, axis=1)
            acc = acc + jnp.sum(v.reshape(8, 8, 512), axis=0)
        acc = jnp.sum(acc, axis=0, keepdims=True)
        mine = rsum.at[z, yl]
        for r in range(4):
            mine[r:r + 1, :] = acc[:, r * W:(r + 1) * W]
        mine[4:8, :] = jnp.zeros((4, W), jnp.float32)
        copies = []
        for dz in range(NZ):
            for dy in range(NL):
                if dz or dy:
                    copies.append(remote(
                        mine, mine, rs_s.at[dz, dy], rs_r.at[dz, dy],
                        device(x, (z + dz) % NZ, (yl + dy) % NL, yh, c)))
                    copies[-1].start()
        return copies

    def column_sums():
        def body(i, acc):
            k = x * 8 + i
            v = cn[at(k, W), at(tile, W)].astype(jnp.float32)
            now, lag = v * wcol[at(k, W), :], v * vcol[at(k, W), :]
            return acc + jnp.concatenate(
                [jnp.sum(now.reshape(16, 8, W), axis=0), jnp.sum(lag.reshape(16, 8, W), axis=0)], axis=1)

        acc = lax.fori_loop(0, 8, body, jnp.zeros((8, 2 * W), jnp.float32), unroll=True)
        acc = jnp.sum(acc, axis=0, keepdims=True)
        mine = csum.at[tile, x]
        mine[0:1, :] = acc[:, :W]
        mine[1:2, :] = acc[:, W:]
        mine[2:8, :] = jnp.zeros((6, W), jnp.float32)
        copies = []
        for dx in range(NX):
            for dh in range(2):
                for dc in range(2):
                    if dx or dh or dc:
                        copies.append(remote(
                            mine, mine, cs_s.at[dx, dh * 2 + dc], cs_r.at[dx, dh * 2 + dc],
                            device((x + dx) % NX, z, yl, (yh + dh) % 2, (c + dc) % 2)))
                        copies[-1].start()
        return copies

    def center_columns(t, xs):
        means = cmean[t]
        now, lag = means[0:1, :], means[1:2, :]
        for i in range(8):
            frames = at(xs * 8 + i, W)
            v = cn[frames, at(t, W)].astype(jnp.float32)
            ul[frames, at(t, W)] = (v - now).astype(jnp.bfloat16)
            vl[frames, at(t, W)] = (v - lag).astype(jnp.bfloat16)

    def lagged_columns(lo, hi):
        def body(i, _):
            v = vl[pl.ds(pl.multiple_of(i * W, W), 2 * W), :]
            lagged = jnp.dot(pick[at(i, W), :], v, preferred_element_type=jnp.float32)
            ul[at(i, W), pl.ds(512, 512)] = lagged.astype(jnp.bfloat16)
            return 0

        lax.fori_loop(lo, hi, body, 0, unroll=4)

    def out_copy(j, w, dx):
        tx = (x + dx) % NX
        dst = out_ref.at[x * 4 + j, w]
        if dx == 0:
            return pltpu.make_async_copy(outb.at[j, tx, w], dst, keep_sem.at[j, w])
        return remote(outb.at[j, tx, w], dst, out_s.at[j, w, dx], out_r.at[j, w, dx], device(tx, z, yl, yh, c))

    def encode(j, t, w, v):
        size = jnp.abs(v)
        top = jnp.maximum(jnp.max(jnp.max(size, axis=1, keepdims=True), axis=0, keepdims=True), 1e-37)
        e = jnp.ceil(jnp.log2(top) + 1e-3)
        y = v * lax.rsqrt(jnp.maximum(size, 1e-37)) * (jnp.exp2(-0.5 * e) * CODE_MAX)
        y = y + jnp.where(v < 0, -0.5, 0.5)
        outb[j, t, w, pl.ds(0, W), :] = y.astype(jnp.int32).astype(jnp.int16)
        e = jnp.where(total > 0, e, CODE_MAX)
        outb[j, t, w, pl.ds(W, 16), :] = jnp.broadcast_to(e, (16, W)).astype(jnp.int32).astype(jnp.int16)

    def multiply(s, w):
        first, chunks = (0, 2) if s == B else (s + 1, 1)
        prod = lax.dot_general(
            rc[:, LANES[s]], ul[:, pl.ds(w * 512, 512)], CONTRACT_FRAMES, preferred_element_type=jnp.float32) / total
        for j in range(chunks):
            for t in range(NX):
                encode(first + j, t, w, prod[j * W:(j + 1) * W, t * W:(t + 1) * W])
        for j in range(chunks):
            for dx in (2, 1, 3, 0):
                out_copy(first + j, w, dx).start()

    own_row.wait()
    for cp in rows_b:
        cp.wait_recv()
    for d in (0, 1):
        ring(B, d, 1).start()
    over_y(0, 0).start()
    for cp in rows_a:
        cp.wait_recv()
    row_parts = row_sums()
    for d in (0, 1):
        ring(A0, d, 1).start()
    own_col.wait()
    for cp in cols_a:
        cp.wait_recv()
    col_parts = column_sums()
    col_y().start()
    for d in (0, 1):
        col_x(d, 0).start()
    col_c(0, 0).start()

    ring_step(B, 1)
    ring_step(A0, 1)
    for cp in row_parts:
        cp.wait_recv()
    rmean[...] = jnp.sum(rsum[...].reshape(NZ * NL, 8, W), axis=0) / total
    center_rows(B, z, yl)
    center_rows(A0, z)
    center_rows(A1, z)
    col_y().wait_recv()
    for d in (0, 1):
        col_x(d, 1).start()
    col_c(1, 0).start()
    ring_step(B, 2)
    center_step(B, 1)
    for cp in col_parts:
        cp.wait_recv()
    cmean[...] = (csum[:, 0] + csum[:, 1] + csum[:, 2] + csum[:, 3]) / total
    center_step(A0, 1)
    ring_step(A0, 2)
    col_step_x(0)
    center_columns(tile, x)
    center_columns(other_tile, x)
    center_step(B, 2)
    ring_step(B, 3)
    for q in range(NX):
        for d in (0, 1):
            ring_a1(q, d, 1).start()
    center_step(A0, 2)
    from_core(0, 0)
    from_core(1, 0)
    from_y(0)
    from_y(1)
    ring_step(A0, 3)
    col_step_x(1)
    center_step(B, 3)
    center_step(A0, 3)
    from_core(0, 1)
    from_core(0, 3)
    ring_step(B, 4)
    ring_step(A0, 4)
    center_step(B, 4)
    center_step(A0, 4)
    from_y(2)
    for d in (0, 1):
        col_forward(d).wait_recv()
        col_c(d, 2).start()
    for d in (0, 1):
        center_columns(other_tile if d else tile, (x + 2) % NX)
    a1_step(1)
    from_core(1, 1)
    from_core(1, 3)
    from_core(0, 2)
    from_core(1, 2)
    multiply(A0, 0)
    a1_step(2)
    center_a1(1)
    from_y(3)
    from_y(4)
    multiply(B, 0)
    a1_step(3)
    lagged_columns(0, 32)
    center_a1(2)
    multiply(A0, 1)
    center_a1(3)
    a1_step(4)
    multiply(B, 1)
    center_a1(4)
    multiply(A1, 0)
    multiply(A1, 1)

    for cp in rows_b + rows_a + cols_a + row_parts + col_parts:
        cp.wait_send()
    for d in (0, 1):
        for s in (B, A0):
            for h in range(1, HOPS[s][d] + 1):
                ring(s, d, h).wait_send()
        for q in range(NX):
            for h in range(1, 5):
                if a1_goes(q, d, h):
                    ring_a1(q, d, h).wait_send()
        for h in range(d, HOPS[B][d] + 1):
            over_y(d, h).wait_send()
        for which in (0, 1):
            col_x(d, which).wait_send()
        col_forward(d).wait_send()
    col_y().wait_send()
    for k in range(4):
        for which in (0, 1):
            col_c(which, k).wait_send()
    for j in range(4):
        for w in (0, 1):
            for dx in range(NX):
                out_copy(j, w, dx).wait()


def decode(code_ref, inst_ref, lag_ref):
    for w, ref in enumerate((inst_ref, lag_ref)):
        for k in range(code_ref.shape[0]):
            e = code_ref[k, w, W:CODE_ROWS, :].astype(jnp.float32)[:1]
            root = code_ref[k, w, :W, :].astype(jnp.float32) * (jnp.exp2(0.5 * e) / CODE_MAX)
            ref[k * W:(k + 1) * W, :] = root * jnp.abs(root)


def shards(frames, partner, usable):
    dma = pltpu.SemaphoreType.DMA
    blocks = frames.shape[1] // W
    out = jax.ShapeDtypeStruct((blocks, 2, CODE_ROWS, W), jnp.int16)
    anywhere = pl.BlockSpec(memory_space=pl.ANY)
    coded = pl.pallas_call(
        kernel,
        out_shape=out,
        in_specs=[anywhere] * 3,
        out_specs=anywhere,
        scratch_shapes=[
            pltpu.VMEM((BLOCKS, W), jnp.int32),
            pltpu.VMEM((BLOCKS, W), jnp.int32),
            pltpu.VMEM((64, 2048), jnp.bfloat16),
            pltpu.VMEM((NX, NZ, W, 512), jnp.bfloat16),
            pltpu.VMEM((FRAMES, 512), jnp.bfloat16),
            pltpu.VMEM((FRAMES, 512), jnp.bfloat16),
            pltpu.VMEM((FRAMES + W, 512), jnp.bfloat16),
            pltpu.VMEM((FRAMES, 1024), jnp.bfloat16),
            pltpu.VMEM((FRAMES, 2 * W), jnp.bfloat16),
            pltpu.VMEM((FRAMES, W), jnp.float32),
            pltpu.VMEM((FRAMES, W), jnp.float32),
            pltpu.VMEM((4, NX, 2, CODE_ROWS, W), jnp.int16),
            pltpu.VMEM((BLOCKS, W), jnp.float32),
            pltpu.VMEM((NZ, NL, 8, W), jnp.float32),
            pltpu.VMEM((4, NX, 8, W), jnp.float32),
            pltpu.VMEM((8, W), jnp.float32),
            pltpu.VMEM((4, 8, W), jnp.float32),
            dma((3,)), dma((2,)), dma((4,)), dma((4,)), dma((8,)), dma((8,)), dma((16,)), dma((16,)),
            dma((2, 2, 4)), dma((2, 2, 4)), dma((2, NX, 4)), dma((2, NX, 4)), dma((2, 5)), dma((2, 5)),
            dma((NZ, NL)), dma((NZ, NL)), dma((NX, 4)), dma((NX, 4)),
            dma(()), dma(()), dma((2, 2)), dma((2, 2)), dma((2,)), dma((2,)), dma((2, 4)), dma((2, 4)),
            dma((4, 2, NX)), dma((4, 2, NX)), dma((4, 2)),
        ],
        compiler_params=pltpu.CompilerParams(
            collective_id=0, has_side_effects=True, vmem_limit_bytes=56 << 20),
        name="covariances",
    )(partner.reshape(BLOCKS, W), usable.reshape(BLOCKS, W), frames)
    step = blocks // 4
    result = jax.ShapeDtypeStruct((blocks * W, W), jnp.float32)
    spec = pl.BlockSpec((step * W, W), lambda i: (i, 0))
    return pl.pallas_call(
        decode,
        grid=(blocks // step,),
        out_shape=(result, result),
        in_specs=[pl.BlockSpec((step, 2, CODE_ROWS, W), lambda i: (i, 0, 0, 0))],
        out_specs=(spec, spec),
        name="decode",
    )(coded)


def solution(mesh):
    in_specs = (P("tm", "tile"), P(), P())
    out_specs = (P("tile", "tm"), P("tile", "tm"))
    return jax.shard_map(shards, mesh=mesh, in_specs=in_specs, out_specs=out_specs, check_vma=False)
```

```python
import jax
import jax.numpy as jnp
from jax import lax
from jax.experimental import pallas as pl
from jax.experimental.pallas import tpu as pltpu
from jax.sharding import PartitionSpec as P

MESH = pl.DeviceIdType.MESH
NX, NZ, NL = 4, 8, 2
W = 128
LAG = 16
BLOCKS = NX * NZ
FRAMES = BLOCKS * W
CONTRACT_FRAMES = (((0,), (0,)), ((), ()))
B, A0, A1 = range(3)
HOPS = ((4, 3), (3, 4))
LANES = (pl.ds(0, 256), pl.ds(256, W), pl.ds(384, W))
CODE_ROWS = W + 16
CODE_MAX = 32767.0


def coords():
    tm, tile = lax.axis_index("tm"), lax.axis_index("tile")
    return tm // (NZ * NL), (tm // NL) % NZ, tm % NL, tile // 2, tile % 2


def device(x, z, yl, yh, c):
    return (x * (NZ * NL) + z * NL + yl, yh * 2 + c)


def at(index, size):
    return pl.ds(pl.multiple_of(index * size, size), size)


def kernel(
    partner_hbm, usable_hbm, frames_hbm, out_ref,
    partner_ref, usable_ref, frames_ref, row, rc, cn, vl, ul, pick, wcol, vcol, outb, vrow, rsum, csum, rmean, cmean,
    in_sem, own_sem, rb_s, rb_r, ra_s, ra_r, ca_s, ca_r, ring_s, ring_r, a1_s, a1_r, fy_s, fy_r, rs_s, rs_r, cs_s, cs_r,
    cy_s, cy_r, cx_s, cx_r, cf_s, cf_r, cc_s, cc_r, out_s, out_r, keep_sem,
):
    x, z, yl, yh, c = coords()
    tile = yh * 2 + c
    other_tile = (1 - yh) * 2 + c

    def remote(src, dst, send, recv, dev):
        return pltpu.make_async_remote_copy(
            src_ref=src, dst_ref=dst, send_sem=send, recv_sem=recv, device_id=dev, device_id_type=MESH)

    fetch = [
        pltpu.make_async_copy(frames_hbm, frames_ref, in_sem.at[0]),
        pltpu.make_async_copy(usable_hbm, usable_ref, in_sem.at[1]),
        pltpu.make_async_copy(partner_hbm, partner_ref, in_sem.at[2]),
    ]
    for cp in fetch:
        cp.start()
    peers = []
    for dx in range(NX):
        for dy in range(NL):
            if dx or dy:
                peers.append(device((x + dx) % NX, z, (yl + dy) % NL, yh, c))
    for dz in range(1, NZ):
        for dy in range(NL):
            peers.append(device(x, (z + dz) % NZ, (yl + dy) % NL, yh, c))
    for dx in range(NX):
        for dh in range(2):
            for dc in range(2):
                if dh or dc:
                    peers.append(device((x + dx) % NX, z, yl, (yh + dh) % 2, (c + dc) % 2))
    barrier = pltpu.get_barrier_semaphore()
    for p in peers:
        pl.semaphore_signal(barrier, inc=1, device_id=p, device_id_type=MESH)

    def piece(t, xs):
        return cn.at[at(xs, 1024), at(t, W)]

    my_block = z * NL + yl
    my_rows = row.at[x, z, at(yl, 64), :]
    my_cols = cn.at[at(x * 16 + my_block, 64), at(tile, W)]
    fetch[0].wait()
    own_row = pltpu.make_async_copy(frames_ref.at[:, at(x, 512)], my_rows, own_sem.at[0])
    own_row.start()
    own_col = pltpu.make_async_copy(frames_ref.at[:, at(my_block, W)], my_cols, own_sem.at[1])
    own_col.start()
    pl.semaphore_wait(barrier, len(peers))

    rows_b, rows_a, cols_a = [], [], []
    for dx in range(1, NX):
        tx = (x + dx) % NX
        rows_b.append(remote(
            frames_ref.at[:, at(tx * 2, 256)], row.at[x, z, at(yl, 64), pl.ds(0, 256)],
            rb_s.at[dx], rb_r.at[dx], device(tx, z, yl, yh, c)))
        rows_b[-1].start()
    for dx in range(NX):
        for dy in range(NL):
            if dx or dy:
                tx, k = (x + dx) % NX, dx * NL + dy
                rows_a.append(remote(
                    frames_ref.at[:, at(tx * 2 + 1, 256)], row.at[x, z, at(yl, 64), pl.ds(256, 256)],
                    ra_s.at[k], ra_r.at[k], device(tx, z, (yl + dy) % NL, yh, c)))
                rows_a[-1].start()
    for dz in range(NZ):
        for dy in range(NL):
            if dz or dy:
                tz, ty, k = (z + dz) % NZ, (yl + dy) % NL, dz * NL + dy
                cols_a.append(remote(
                    frames_ref.at[:, at(tz * NL + ty, W)], my_cols,
                    ca_s.at[k], ca_r.at[k], device(x, tz, ty, yh, c)))
                cols_a[-1].start()

    fetch[1].wait()
    fetch[2].wait()
    total = jnp.sum(usable_ref[...].astype(jnp.float32))

    ahead = partner_ref[...] - (
        lax.broadcasted_iota(jnp.int32, (BLOCKS, W), 0) * W + lax.broadcasted_iota(jnp.int32, (BLOCKS, W), 1))
    lane = lax.broadcasted_iota(jnp.int32, (BLOCKS, W), 1)
    weight = usable_ref[...].astype(jnp.float32)
    count = jnp.where(ahead == 0, weight, 0.0)
    for k in range(1, LAG + 1):
        r = pltpu.roll(jnp.where(ahead == k, weight, 0.0), k, axis=1)
        count += jnp.where(lane < k, pltpu.roll(r, 1, axis=0), r)
    vrow[...] = count

    def weights(i, _):
        w = usable_ref[pl.ds(i, 1), :].astype(jnp.float32)
        wcol[at(i, W), :] = jnp.broadcast_to(w, (W, W)).T
        vcol[at(i, W), :] = jnp.broadcast_to(vrow[pl.ds(i, 1), :], (W, W)).T
        return 0

    lax.fori_loop(0, BLOCKS, weights, 0, unroll=4)

    def picks(i, _):
        p = (partner_ref[pl.ds(i, 1), :] - i * W).astype(jnp.float32)
        p = jnp.broadcast_to(p, (W, W)).T
        s = lax.broadcasted_iota(jnp.int32, (W, 2 * W), 1).astype(jnp.float32)
        pick[at(i, W), :] = jnp.where(s == jnp.concatenate([p, p], axis=1), 1.0, 0.0).astype(jnp.bfloat16)
        return 0

    lax.fori_loop(0, BLOCKS, picks, 0, unroll=2)
    vl[pl.ds(FRAMES, W), :] = jnp.zeros((W, 512), jnp.bfloat16)

    def behind(d, h):
        return (z + (NZ - h if d == 0 else h)) % NZ

    def ahead_z(d):
        return device(x, (z + (1 if d == 0 else NZ - 1)) % NZ, yl, yh, c)

    def ring(s, d, h):
        frames = at(yl, 64) if s == B else slice(None)
        ref = row.at[:, behind(d, h - 1), frames, LANES[s]]
        return remote(ref, ref, ring_s.at[d, s, h - 1], ring_r.at[d, s, h - 1], ahead_z(d))

    def ring_a1(q, d, h):
        ref = row.at[pl.ds(2 * q, 2), behind(d, h - 1), :, LANES[A1]]
        return remote(ref, ref, a1_s.at[d, q, h - 1], a1_r.at[d, q, h - 1], ahead_z(d))

    def over_y(d, h):
        ref = row.at[:, behind(d, h), at(yl, 64), LANES[B]]
        return remote(ref, ref, fy_s.at[d, h], fy_r.at[d, h], device(x, z, 1 - yl, yh, c))

    def center_rows(s, blk, half=None, only=None):
        lo = 0 if s == B else s + 1
        mean = rmean[lo:lo + 1, :]
        if s == B:
            mean = jnp.concatenate([mean, rmean[1:2, :]], axis=1)
        for q in range(NX) if only is None else (2 * only, 2 * only + 1):
            base = (q * NZ + blk) * 2
            frames, inner = (at(base // 2, W), slice(None)) if half is None else (at(base + half, 64), at(half, 64))
            v = row[q, blk, inner, LANES[s]].astype(jnp.float32)
            w = wcol[frames, :]
            if s == B:
                w = jnp.concatenate([w, w], axis=1)
            rc[frames, LANES[s]] = ((v - mean) * w).astype(jnp.bfloat16)

    def ring_step(s, h):
        for d in (0, 1):
            if h <= HOPS[s][d]:
                ring(s, d, h).wait_recv()
                if h < HOPS[s][d]:
                    ring(s, d, h + 1).start()
                if s == B:
                    over_y(d, h).start()

    def center_step(s, h):
        for d in (0, 1):
            if h <= HOPS[s][d]:
                center_rows(s, behind(d, h), yl if s == B else None)

    def from_y(h):
        for d in (0, 1):
            if d <= h <= HOPS[B][d]:
                over_y(d, h).wait_recv()
                center_rows(B, behind(d, h), 1 - yl)

    def a1_goes(q, d, h):
        return h < 4 or q == d

    def a1_step(h):
        for q in range(2):
            for d in (0, 1):
                if a1_goes(q, d, h):
                    ring_a1(q, d, h).wait_recv()
                    if h < 4 and a1_goes(q, d, h + 1):
                        ring_a1(q, d, h + 1).start()

    def center_a1(h):
        for q in range(2):
            for d in (0, 1):
                if a1_goes(q, d, h):
                    center_rows(A1, behind(d, h), only=q)

    def col_y():
        ref = piece(tile, x)
        return remote(ref, ref, cy_s, cy_r, device(x, z, yl, 1 - yh, c))

    def col_x(d, which):
        ref = piece(other_tile if which else tile, x)
        return remote(ref, ref, cx_s.at[d, which], cx_r.at[d, which],
                      device((x + (1 if d == 0 else NX - 1)) % NX, z, yl, yh, c))

    def col_forward(d):
        step = 1 if d == 0 else NX - 1
        ref = piece(other_tile if d else tile, (x + NX - step) % NX)
        return remote(ref, ref, cf_s.at[d], cf_r.at[d], device((x + step) % NX, z, yl, yh, c))

    def col_c(which, k):
        ref = piece(other_tile if which else tile, (x + k) % NX)
        return remote(ref, ref, cc_s.at[which, k], cc_r.at[which, k], device(x, z, yl, yh, 1 - c))

    def col_step_x(which):
        for d in (0, 1):
            col_x(d, which).wait_recv()
            if which == d:
                col_forward(d).start()
            col_c(which, NX - 1 if d == 0 else 1).start()

    def center_x(which):
        for k in (NX - 1, 1):
            center_columns(other_tile if which else tile, (x + k) % NX)

    def from_core(which, k):
        col_c(which, k).wait_recv()
        center_columns((1 - yh if which else yh) * 2 + 1 - c, (x + k) % NX)

    def row_sums():
        acc = jnp.zeros((8, 512), jnp.float32)
        for q in range(NX):
            v = row[q, z, at(yl, 64), :].astype(jnp.float32)
            w = wcol[at((q * NZ + z) * 2 + yl, 64), :]
            v = v * jnp.concatenate([w] * 4, axis=1)
            acc = acc + jnp.sum(v.reshape(8, 8, 512), axis=0)
        acc = jnp.sum(acc, axis=0, keepdims=True)
        mine = rsum.at[z, yl]
        for r in range(4):
            mine[r:r + 1, :] = acc[:, r * W:(r + 1) * W]
        mine[4:8, :] = jnp.zeros((4, W), jnp.float32)
        copies = []
        for dz in range(NZ):
            for dy in range(NL):
                if dz or dy:
                    copies.append(remote(
                        mine, mine, rs_s.at[dz, dy], rs_r.at[dz, dy],
                        device(x, (z + dz) % NZ, (yl + dy) % NL, yh, c)))
                    copies[-1].start()
        return copies

    def column_sums():
        def body(i, acc):
            k = x * 8 + i
            v = cn[at(k, W), at(tile, W)].astype(jnp.float32)
            now, lag = v * wcol[at(k, W), :], v * vcol[at(k, W), :]
            return acc + jnp.concatenate(
                [jnp.sum(now.reshape(16, 8, W), axis=0), jnp.sum(lag.reshape(16, 8, W), axis=0)], axis=1)

        acc = lax.fori_loop(0, 8, body, jnp.zeros((8, 2 * W), jnp.float32), unroll=True)
        acc = jnp.sum(acc, axis=0, keepdims=True)
        mine = csum.at[tile, x]
        mine[0:1, :] = acc[:, :W]
        mine[1:2, :] = acc[:, W:]
        mine[2:8, :] = jnp.zeros((6, W), jnp.float32)
        copies = []
        for dx in range(NX):
            for dh in range(2):
                for dc in range(2):
                    if dx or dh or dc:
                        copies.append(remote(
                            mine, mine, cs_s.at[dx, dh * 2 + dc], cs_r.at[dx, dh * 2 + dc],
                            device((x + dx) % NX, z, yl, (yh + dh) % 2, (c + dc) % 2)))
                        copies[-1].start()
        return copies

    def center_columns(t, xs):
        means = cmean[t]
        now, lag = means[0:1, :], means[1:2, :]
        for i in range(8):
            frames = at(xs * 8 + i, W)
            v = cn[frames, at(t, W)].astype(jnp.float32)
            ul[frames, at(t, W)] = (v - now).astype(jnp.bfloat16)
            vl[frames, at(t, W)] = (v - lag).astype(jnp.bfloat16)

    def lagged_columns(lo, hi):
        def body(i, _):
            v = vl[pl.ds(pl.multiple_of(i * W, W), 2 * W), :]
            lagged = jnp.dot(pick[at(i, W), :], v, preferred_element_type=jnp.float32)
            ul[at(i, W), pl.ds(512, 512)] = lagged.astype(jnp.bfloat16)
            return 0

        lax.fori_loop(lo, hi, body, 0, unroll=4)

    def out_copy(j, w, dx):
        tx = (x + dx) % NX
        dst = out_ref.at[x * 4 + j, w]
        if dx == 0:
            return pltpu.make_async_copy(outb.at[j, tx, w], dst, keep_sem.at[j, w])
        return remote(outb.at[j, tx, w], dst, out_s.at[j, w, dx], out_r.at[j, w, dx], device(tx, z, yl, yh, c))

    def encode(j, t, w, v):
        size = jnp.abs(v)
        top = jnp.maximum(jnp.max(jnp.max(size, axis=1, keepdims=True), axis=0, keepdims=True), 1e-37)
        e = jnp.ceil(jnp.log2(top) + 1e-3)
        y = v * lax.rsqrt(jnp.maximum(size, 1e-37)) * (jnp.exp2(-0.5 * e) * CODE_MAX)
        y = y + jnp.where(v < 0, -0.5, 0.5)
        outb[j, t, w, pl.ds(0, W), :] = y.astype(jnp.int32).astype(jnp.int16)
        e = jnp.where(total > 0, e, CODE_MAX)
        outb[j, t, w, pl.ds(W, 16), :] = jnp.broadcast_to(e, (16, W)).astype(jnp.int32).astype(jnp.int16)

    def multiply(s, w):
        first, chunks = (0, 2) if s == B else (s + 1, 1)
        prod = lax.dot_general(
            rc[:, LANES[s]], ul[:, pl.ds(w * 512, 512)], CONTRACT_FRAMES, preferred_element_type=jnp.float32) / total
        for j in range(chunks):
            for t in range(NX):
                encode(first + j, t, w, prod[j * W:(j + 1) * W, t * W:(t + 1) * W])
        for j in range(chunks):
            for dx in (2, 1, 3, 0):
                out_copy(first + j, w, dx).start()

    own_row.wait()
    for cp in rows_b:
        cp.wait_recv()
    for d in (0, 1):
        ring(B, d, 1).start()
    over_y(0, 0).start()
    for cp in rows_a:
        cp.wait_recv()
    row_parts = row_sums()
    for d in (0, 1):
        ring(A0, d, 1).start()
    own_col.wait()
    for cp in cols_a:
        cp.wait_recv()
    col_parts = column_sums()
    col_y().start()
    for d in (0, 1):
        col_x(d, 0).start()
    col_c(0, 0).start()

    ring_step(B, 1)
    ring_step(A0, 1)
    for q in (0, 1):
        for d in (0, 1):
            ring_a1(q, d, 1).start()
    col_y().wait_recv()
    for d in (0, 1):
        col_x(d, 1).start()
    col_c(1, 0).start()
    col_step_x(0)
    ring_step(B, 2)
    for cp in row_parts:
        cp.wait_recv()
    rmean[...] = jnp.sum(rsum[...].reshape(NZ * NL, 8, W), axis=0) / total
    center_rows(B, z, yl)
    center_step(B, 1)
    center_rows(A0, z)
    center_step(A0, 1)
    ring_step(A0, 2)
    for cp in col_parts:
        cp.wait_recv()
    cmean[...] = (csum[:, 0] + csum[:, 1] + csum[:, 2] + csum[:, 3]) / total
    center_columns(tile, x)
    col_step_x(1)
    a1_step(1)
    center_columns(other_tile, x)
    center_x(0)
    center_rows(A1, z)
    center_step(B, 2)
    ring_step(B, 3)
    center_x(1)
    center_step(A0, 2)
    for d in (0, 1):
        col_forward(d).wait_recv()
        col_c(d, 2).start()
    ring_step(A0, 3)
    for d in (0, 1):
        center_columns(other_tile if d else tile, (x + 2) % NX)
    center_a1(1)
    from_core(0, 0)
    from_core(1, 0)
    from_core(0, 1)
    from_core(0, 3)
    from_y(0)
    from_y(1)
    center_step(B, 3)
    center_step(A0, 3)
    a1_step(2)
    center_a1(2)
    from_core(1, 1)
    from_core(1, 3)
    from_y(2)
    ring_step(B, 4)
    ring_step(A0, 4)
    center_step(B, 4)
    center_step(A0, 4)
    from_core(0, 2)
    from_core(1, 2)
    multiply(A0, 0)
    a1_step(3)
    from_y(3)
    from_y(4)
    multiply(B, 0)
    lagged_columns(0, 32)
    center_a1(3)
    multiply(A0, 1)
    multiply(B, 1)
    a1_step(4)
    center_a1(4)
    multiply(A1, 0)
    multiply(A1, 1)

    for cp in rows_b + rows_a + cols_a + row_parts + col_parts:
        cp.wait_send()
    for d in (0, 1):
        for s in (B, A0):
            for h in range(1, HOPS[s][d] + 1):
                ring(s, d, h).wait_send()
        for q in range(2):
            for h in range(1, 5):
                if a1_goes(q, d, h):
                    ring_a1(q, d, h).wait_send()
        for h in range(d, HOPS[B][d] + 1):
            over_y(d, h).wait_send()
        for which in (0, 1):
            col_x(d, which).wait_send()
        col_forward(d).wait_send()
    col_y().wait_send()
    for k in range(4):
        for which in (0, 1):
            col_c(which, k).wait_send()
    for j in range(4):
        for w in (0, 1):
            for dx in range(NX):
                out_copy(j, w, dx).wait()


def decode(code_ref, inst_ref, lag_ref):
    for w, ref in enumerate((inst_ref, lag_ref)):
        for k in range(code_ref.shape[0]):
            e = code_ref[k, w, W:CODE_ROWS, :].astype(jnp.float32)[:1]
            root = code_ref[k, w, :W, :].astype(jnp.float32) * (jnp.exp2(0.5 * e) / CODE_MAX)
            ref[k * W:(k + 1) * W, :] = root * jnp.abs(root)


def shards(frames, partner, usable):
    dma = pltpu.SemaphoreType.DMA
    blocks = frames.shape[1] // W
    out = jax.ShapeDtypeStruct((blocks, 2, CODE_ROWS, W), jnp.int16)
    anywhere = pl.BlockSpec(memory_space=pl.ANY)
    coded = pl.pallas_call(
        kernel,
        out_shape=out,
        in_specs=[anywhere] * 3,
        out_specs=anywhere,
        scratch_shapes=[
            pltpu.VMEM((BLOCKS, W), jnp.int32),
            pltpu.VMEM((BLOCKS, W), jnp.int32),
            pltpu.VMEM((64, 2048), jnp.bfloat16),
            pltpu.VMEM((NX, NZ, W, 512), jnp.bfloat16),
            pltpu.VMEM((FRAMES, 512), jnp.bfloat16),
            pltpu.VMEM((FRAMES, 512), jnp.bfloat16),
            pltpu.VMEM((FRAMES + W, 512), jnp.bfloat16),
            pltpu.VMEM((FRAMES, 1024), jnp.bfloat16),
            pltpu.VMEM((FRAMES, 2 * W), jnp.bfloat16),
            pltpu.VMEM((FRAMES, W), jnp.float32),
            pltpu.VMEM((FRAMES, W), jnp.float32),
            pltpu.VMEM((4, NX, 2, CODE_ROWS, W), jnp.int16),
            pltpu.VMEM((BLOCKS, W), jnp.float32),
            pltpu.VMEM((NZ, NL, 8, W), jnp.float32),
            pltpu.VMEM((4, NX, 8, W), jnp.float32),
            pltpu.VMEM((8, W), jnp.float32),
            pltpu.VMEM((4, 8, W), jnp.float32),
            dma((3,)), dma((2,)), dma((4,)), dma((4,)), dma((8,)), dma((8,)), dma((16,)), dma((16,)),
            dma((2, 2, 4)), dma((2, 2, 4)), dma((2, 2, 4)), dma((2, 2, 4)), dma((2, 5)), dma((2, 5)),
            dma((NZ, NL)), dma((NZ, NL)), dma((NX, 4)), dma((NX, 4)),
            dma(()), dma(()), dma((2, 2)), dma((2, 2)), dma((2,)), dma((2,)), dma((2, 4)), dma((2, 4)),
            dma((4, 2, NX)), dma((4, 2, NX)), dma((4, 2)),
        ],
        compiler_params=pltpu.CompilerParams(
            collective_id=0, has_side_effects=True, vmem_limit_bytes=56 << 20),
        name="covariances",
    )(partner.reshape(BLOCKS, W), usable.reshape(BLOCKS, W), frames)
    step = blocks // 2
    result = jax.ShapeDtypeStruct((blocks * W, W), jnp.float32)
    spec = pl.BlockSpec((step * W, W), lambda i: (i, 0))
    return pl.pallas_call(
        decode,
        grid=(blocks // step,),
        out_shape=(result, result),
        in_specs=[pl.BlockSpec((step, 2, CODE_ROWS, W), lambda i: (i, 0, 0, 0))],
        out_specs=(spec, spec),
        name="decode",
    )(coded)


def solution(mesh):
    in_specs = (P("tm", "tile"), P(), P())
    out_specs = (P("tile", "tm"), P("tile", "tm"))
    return jax.shard_map(shards, mesh=mesh, in_specs=in_specs, out_specs=out_specs, check_vma=False)
```

```python
import jax
import jax.numpy as jnp
from jax import lax
from jax.experimental import pallas as pl
from jax.experimental.pallas import tpu as pltpu
from jax.sharding import PartitionSpec as P

MESH = pl.DeviceIdType.MESH
NX, NZ, NL = 4, 8, 2
W = 128
LAG = 16
BLOCKS = NX * NZ
FRAMES = BLOCKS * W
CONTRACT_FRAMES = (((0,), (0,)), ((), ()))
B, A0, A1 = range(3)
HOPS = ((4, 3), (3, 4))
LANES = (pl.ds(0, 256), pl.ds(256, W), pl.ds(384, W))
CODE_ROWS = W + 16
CODE_MAX = 32767.0


def coords():
    tm, tile = lax.axis_index("tm"), lax.axis_index("tile")
    return tm // (NZ * NL), (tm // NL) % NZ, tm % NL, tile // 2, tile % 2


def device(x, z, yl, yh, c):
    return (x * (NZ * NL) + z * NL + yl, yh * 2 + c)


def at(index, size):
    return pl.ds(pl.multiple_of(index * size, size), size)


def kernel(
    partner_hbm, usable_hbm, frames_hbm, out_ref,
    partner_ref, usable_ref, frames_ref, row, rc, cn, vl, ul, pick, wcol, vcol, outb, vrow, rsum, csum, rmean, cmean,
    in_sem, own_sem, rb_s, rb_r, ra_s, ra_r, ca_s, ca_r, ring_s, ring_r, a1_s, a1_r, fy_s, fy_r, rs_s, rs_r, cs_s, cs_r,
    cy_s, cy_r, cx_s, cx_r, cf_s, cf_r, cc_s, cc_r, out_s, out_r, keep_sem,
):
    x, z, yl, yh, c = coords()
    tile = yh * 2 + c
    other_tile = (1 - yh) * 2 + c

    def remote(src, dst, send, recv, dev):
        return pltpu.make_async_remote_copy(
            src_ref=src, dst_ref=dst, send_sem=send, recv_sem=recv, device_id=dev, device_id_type=MESH)

    fetch = [
        pltpu.make_async_copy(frames_hbm, frames_ref, in_sem.at[0]),
        pltpu.make_async_copy(usable_hbm, usable_ref, in_sem.at[1]),
        pltpu.make_async_copy(partner_hbm, partner_ref, in_sem.at[2]),
    ]
    for cp in fetch:
        cp.start()
    peers = []
    for dx in range(NX):
        for dy in range(NL):
            if dx or dy:
                peers.append(device((x + dx) % NX, z, (yl + dy) % NL, yh, c))
    for dz in range(1, NZ):
        for dy in range(NL):
            peers.append(device(x, (z + dz) % NZ, (yl + dy) % NL, yh, c))
    for dx in range(NX):
        for dh in range(2):
            for dc in range(2):
                if dh or dc:
                    peers.append(device((x + dx) % NX, z, yl, (yh + dh) % 2, (c + dc) % 2))
    barrier = pltpu.get_barrier_semaphore()
    for p in peers:
        pl.semaphore_signal(barrier, inc=1, device_id=p, device_id_type=MESH)

    def piece(t, xs):
        return cn.at[at(xs, 1024), at(t, W)]

    my_block = z * NL + yl
    my_rows = row.at[x, z, at(yl, 64), :]
    my_cols = cn.at[at(x * 16 + my_block, 64), at(tile, W)]
    fetch[0].wait()
    own_row = pltpu.make_async_copy(frames_ref.at[:, at(x, 512)], my_rows, own_sem.at[0])
    own_row.start()
    own_col = pltpu.make_async_copy(frames_ref.at[:, at(my_block, W)], my_cols, own_sem.at[1])
    own_col.start()
    pl.semaphore_wait(barrier, len(peers))

    rows_b, rows_a, cols_a = [], [], []
    for dx in range(1, NX):
        tx = (x + dx) % NX
        rows_b.append(remote(
            frames_ref.at[:, at(tx * 2, 256)], row.at[x, z, at(yl, 64), pl.ds(0, 256)],
            rb_s.at[dx], rb_r.at[dx], device(tx, z, yl, yh, c)))
        rows_b[-1].start()
    for dx in range(NX):
        for dy in range(NL):
            if dx or dy:
                tx, k = (x + dx) % NX, dx * NL + dy
                rows_a.append(remote(
                    frames_ref.at[:, at(tx * 2 + 1, 256)], row.at[x, z, at(yl, 64), pl.ds(256, 256)],
                    ra_s.at[k], ra_r.at[k], device(tx, z, (yl + dy) % NL, yh, c)))
                rows_a[-1].start()
    for dz in range(NZ):
        for dy in range(NL):
            if dz or dy:
                tz, ty, k = (z + dz) % NZ, (yl + dy) % NL, dz * NL + dy
                cols_a.append(remote(
                    frames_ref.at[:, at(tz * NL + ty, W)], my_cols,
                    ca_s.at[k], ca_r.at[k], device(x, tz, ty, yh, c)))
                cols_a[-1].start()

    fetch[1].wait()
    fetch[2].wait()
    total = jnp.sum(usable_ref[...].astype(jnp.float32))

    ahead = partner_ref[...] - (
        lax.broadcasted_iota(jnp.int32, (BLOCKS, W), 0) * W + lax.broadcasted_iota(jnp.int32, (BLOCKS, W), 1))
    lane = lax.broadcasted_iota(jnp.int32, (BLOCKS, W), 1)
    weight = usable_ref[...].astype(jnp.float32)
    count = jnp.where(ahead == 0, weight, 0.0)
    for k in range(1, LAG + 1):
        r = pltpu.roll(jnp.where(ahead == k, weight, 0.0), k, axis=1)
        count += jnp.where(lane < k, pltpu.roll(r, 1, axis=0), r)
    vrow[...] = count

    def weights(i, _):
        w = usable_ref[pl.ds(i, 1), :].astype(jnp.float32)
        wcol[at(i, W), :] = jnp.broadcast_to(w, (W, W)).T
        vcol[at(i, W), :] = jnp.broadcast_to(vrow[pl.ds(i, 1), :], (W, W)).T
        return 0

    lax.fori_loop(0, BLOCKS, weights, 0, unroll=4)

    def picks(i, _):
        p = (partner_ref[pl.ds(i, 1), :] - i * W).astype(jnp.float32)
        p = jnp.broadcast_to(p, (W, W)).T
        s = lax.broadcasted_iota(jnp.int32, (W, 2 * W), 1).astype(jnp.float32)
        pick[at(i, W), :] = jnp.where(s == jnp.concatenate([p, p], axis=1), 1.0, 0.0).astype(jnp.bfloat16)
        return 0

    lax.fori_loop(0, BLOCKS, picks, 0, unroll=2)
    vl[pl.ds(FRAMES, W), :] = jnp.zeros((W, 512), jnp.bfloat16)

    def behind(d, h):
        return (z + (NZ - h if d == 0 else h)) % NZ

    def ahead_z(d):
        return device(x, (z + (1 if d == 0 else NZ - 1)) % NZ, yl, yh, c)

    def ring(s, d, h):
        frames = at(yl, 64) if s == B else slice(None)
        ref = row.at[:, behind(d, h - 1), frames, LANES[s]]
        return remote(ref, ref, ring_s.at[d, s, h - 1], ring_r.at[d, s, h - 1], ahead_z(d))

    def ring_a1(q, d, h):
        ref = row.at[pl.ds(2 * q, 2), behind(d, h - 1), :, LANES[A1]]
        return remote(ref, ref, a1_s.at[d, q, h - 1], a1_r.at[d, q, h - 1], ahead_z(d))

    def over_y(d, h):
        ref = row.at[:, behind(d, h), at(yl, 64), LANES[B]]
        return remote(ref, ref, fy_s.at[d, h], fy_r.at[d, h], device(x, z, 1 - yl, yh, c))

    def center_rows(s, blk, half=None, only=None):
        lo = 0 if s == B else s + 1
        mean = rmean[lo:lo + 1, :]
        if s == B:
            mean = jnp.concatenate([mean, rmean[1:2, :]], axis=1)
        for q in range(NX) if only is None else (2 * only, 2 * only + 1):
            base = (q * NZ + blk) * 2
            frames, inner = (at(base // 2, W), slice(None)) if half is None else (at(base + half, 64), at(half, 64))
            v = row[q, blk, inner, LANES[s]].astype(jnp.float32)
            w = wcol[frames, :]
            if s == B:
                w = jnp.concatenate([w, w], axis=1)
            rc[frames, LANES[s]] = ((v - mean) * w).astype(jnp.bfloat16)

    def ring_step(s, h):
        for d in (0, 1):
            if h <= HOPS[s][d]:
                ring(s, d, h).wait_recv()
                if h < HOPS[s][d]:
                    ring(s, d, h + 1).start()
                if s == B:
                    over_y(d, h).start()

    def center_step(s, h):
        for d in (0, 1):
            if h <= HOPS[s][d]:
                center_rows(s, behind(d, h), yl if s == B else None)

    def from_y(h):
        for d in (0, 1):
            if d <= h <= HOPS[B][d]:
                over_y(d, h).wait_recv()
                center_rows(B, behind(d, h), 1 - yl)

    def a1_goes(q, d, h):
        return h < 4 or q == d

    def a1_step(h):
        for q in range(2):
            for d in (0, 1):
                if a1_goes(q, d, h):
                    ring_a1(q, d, h).wait_recv()
                    if h < 4 and a1_goes(q, d, h + 1):
                        ring_a1(q, d, h + 1).start()

    def center_a1(h):
        for q in range(2):
            for d in (0, 1):
                if a1_goes(q, d, h):
                    center_rows(A1, behind(d, h), only=q)

    def col_y():
        ref = piece(tile, x)
        return remote(ref, ref, cy_s, cy_r, device(x, z, yl, 1 - yh, c))

    def col_x(d, which):
        ref = piece(other_tile if which else tile, x)
        return remote(ref, ref, cx_s.at[d, which], cx_r.at[d, which],
                      device((x + (1 if d == 0 else NX - 1)) % NX, z, yl, yh, c))

    def col_forward(d):
        step = 1 if d == 0 else NX - 1
        ref = piece(other_tile if d else tile, (x + NX - step) % NX)
        return remote(ref, ref, cf_s.at[d], cf_r.at[d], device((x + step) % NX, z, yl, yh, c))

    def col_c(which, k):
        ref = piece(other_tile if which else tile, (x + k) % NX)
        return remote(ref, ref, cc_s.at[which, k], cc_r.at[which, k], device(x, z, yl, yh, 1 - c))

    def col_step_x(which):
        for d in (0, 1):
            col_x(d, which).wait_recv()
            if which == d:
                col_forward(d).start()
            col_c(which, NX - 1 if d == 0 else 1).start()

    def center_x(which):
        for k in (NX - 1, 1):
            center_columns(other_tile if which else tile, (x + k) % NX)

    def from_core(which, k):
        col_c(which, k).wait_recv()
        center_columns((1 - yh if which else yh) * 2 + 1 - c, (x + k) % NX)

    def row_sums():
        acc = jnp.zeros((8, 512), jnp.float32)
        for q in range(NX):
            v = row[q, z, at(yl, 64), :].astype(jnp.float32)
            w = wcol[at((q * NZ + z) * 2 + yl, 64), :]
            v = v * jnp.concatenate([w] * 4, axis=1)
            acc = acc + jnp.sum(v.reshape(8, 8, 512), axis=0)
        acc = jnp.sum(acc, axis=0, keepdims=True)
        mine = rsum.at[z, yl]
        for r in range(4):
            mine[r:r + 1, :] = acc[:, r * W:(r + 1) * W]
        mine[4:8, :] = jnp.zeros((4, W), jnp.float32)
        copies = []
        for dz in range(NZ):
            for dy in range(NL):
                if dz or dy:
                    copies.append(remote(
                        mine, mine, rs_s.at[dz, dy], rs_r.at[dz, dy],
                        device(x, (z + dz) % NZ, (yl + dy) % NL, yh, c)))
                    copies[-1].start()
        return copies

    def column_sums():
        def body(i, acc):
            k = x * 8 + i
            v = cn[at(k, W), at(tile, W)].astype(jnp.float32)
            now, lag = v * wcol[at(k, W), :], v * vcol[at(k, W), :]
            return acc + jnp.concatenate(
                [jnp.sum(now.reshape(16, 8, W), axis=0), jnp.sum(lag.reshape(16, 8, W), axis=0)], axis=1)

        acc = lax.fori_loop(0, 8, body, jnp.zeros((8, 2 * W), jnp.float32), unroll=True)
        acc = jnp.sum(acc, axis=0, keepdims=True)
        mine = csum.at[tile, x]
        mine[0:1, :] = acc[:, :W]
        mine[1:2, :] = acc[:, W:]
        mine[2:8, :] = jnp.zeros((6, W), jnp.float32)
        copies = []
        for dx in range(NX):
            for dh in range(2):
                for dc in range(2):
                    if dx or dh or dc:
                        copies.append(remote(
                            mine, mine, cs_s.at[dx, dh * 2 + dc], cs_r.at[dx, dh * 2 + dc],
                            device((x + dx) % NX, z, yl, (yh + dh) % 2, (c + dc) % 2)))
                        copies[-1].start()
        return copies

    def center_columns(t, xs):
        means = cmean[t]
        now, lag = means[0:1, :], means[1:2, :]
        for i in range(8):
            frames = at(xs * 8 + i, W)
            v = cn[frames, at(t, W)].astype(jnp.float32)
            ul[frames, at(t, W)] = (v - now).astype(jnp.bfloat16)
            vl[frames, at(t, W)] = (v - lag).astype(jnp.bfloat16)

    def lagged_columns(xs):
        def body(k, _):
            i = xs * 8 + k
            v = vl[pl.ds(pl.multiple_of(i * W, W), 2 * W), :]
            lagged = jnp.dot(pick[at(i, W), :], v, preferred_element_type=jnp.float32)
            ul[at(i, W), pl.ds(512, 512)] = lagged.astype(jnp.bfloat16)
            return 0

        lax.fori_loop(0, 8, body, 0, unroll=4)

    def out_copy(j, w, dx):
        tx = (x + dx) % NX
        dst = out_ref.at[x * 4 + j, w]
        if dx == 0:
            return pltpu.make_async_copy(outb.at[j, tx, w], dst, keep_sem.at[j, w])
        return remote(outb.at[j, tx, w], dst, out_s.at[j, w, dx], out_r.at[j, w, dx], device(tx, z, yl, yh, c))

    def encode(j, t, w, v):
        size = jnp.abs(v)
        top = jnp.maximum(jnp.max(jnp.max(size, axis=1, keepdims=True), axis=0, keepdims=True), 1e-37)
        e = jnp.ceil(jnp.log2(top) + 1e-3)
        y = v * lax.rsqrt(jnp.maximum(size, 1e-37)) * (jnp.exp2(-0.5 * e) * CODE_MAX)
        y = y + jnp.where(v < 0, -0.5, 0.5)
        outb[j, t, w, pl.ds(0, W), :] = y.astype(jnp.int32).astype(jnp.int16)
        e = jnp.where(total > 0, e, CODE_MAX)
        outb[j, t, w, pl.ds(W, 16), :] = jnp.broadcast_to(e, (16, W)).astype(jnp.int32).astype(jnp.int16)

    def multiply(s, w):
        first, chunks = (0, 2) if s == B else (s + 1, 1)
        prod = lax.dot_general(
            rc[:, LANES[s]], ul[:, pl.ds(w * 512, 512)], CONTRACT_FRAMES, preferred_element_type=jnp.float32) / total
        for j in range(chunks):
            for t in range(NX):
                encode(first + j, t, w, prod[j * W:(j + 1) * W, t * W:(t + 1) * W])
        for j in range(chunks):
            for dx in (2, 1, 3, 0):
                out_copy(first + j, w, dx).start()

    own_row.wait()
    for cp in rows_b:
        cp.wait_recv()
    for d in (0, 1):
        ring(B, d, 1).start()
    over_y(0, 0).start()
    for cp in rows_a:
        cp.wait_recv()
    row_parts = row_sums()
    for d in (0, 1):
        ring(A0, d, 1).start()
    own_col.wait()
    for cp in cols_a:
        cp.wait_recv()
    col_parts = column_sums()
    col_y().start()
    for d in (0, 1):
        col_x(d, 0).start()
    col_c(0, 0).start()

    ring_step(B, 1)
    ring_step(A0, 1)
    for q in (0, 1):
        for d in (0, 1):
            ring_a1(q, d, 1).start()
    col_y().wait_recv()
    for d in (0, 1):
        col_x(d, 1).start()
    col_c(1, 0).start()
    col_step_x(0)
    ring_step(B, 2)
    for cp in row_parts:
        cp.wait_recv()
    rmean[...] = jnp.sum(rsum[...].reshape(NZ * NL, 8, W), axis=0) / total
    center_rows(B, z, yl)
    center_step(B, 1)
    center_rows(A0, z)
    center_step(A0, 1)
    ring_step(A0, 2)
    for cp in col_parts:
        cp.wait_recv()
    cmean[...] = (csum[:, 0] + csum[:, 1] + csum[:, 2] + csum[:, 3]) / total
    center_columns(tile, x)
    col_step_x(1)
    a1_step(1)
    center_columns(other_tile, x)
    center_x(0)
    center_rows(A1, z)
    center_step(B, 2)
    ring_step(B, 3)
    center_x(1)
    center_step(A0, 2)
    for d in (0, 1):
        col_forward(d).wait_recv()
        col_c(d, 2).start()
    ring_step(A0, 3)
    for d in (0, 1):
        center_columns(other_tile if d else tile, (x + 2) % NX)
    center_a1(1)
    from_core(0, 0)
    from_core(1, 0)
    from_core(0, 1)
    from_core(0, 3)
    from_y(0)
    from_y(1)
    center_step(B, 3)
    center_step(A0, 3)
    a1_step(2)
    center_a1(2)
    from_core(1, 1)
    from_core(1, 3)
    from_y(2)
    ring_step(B, 4)
    ring_step(A0, 4)
    center_step(B, 4)
    center_step(A0, 4)
    lagged_columns((x + 3) % NX)
    lagged_columns(x)
    from_core(0, 2)
    from_core(1, 2)
    multiply(A0, 0)
    a1_step(3)
    from_y(3)
    from_y(4)
    multiply(B, 0)
    lagged_columns((x + 1) % NX)
    lagged_columns((x + 2) % NX)
    center_a1(3)
    multiply(A0, 1)
    multiply(B, 1)
    a1_step(4)
    center_a1(4)
    multiply(A1, 0)
    multiply(A1, 1)

    for cp in rows_b + rows_a + cols_a + row_parts + col_parts:
        cp.wait_send()
    for d in (0, 1):
        for s in (B, A0):
            for h in range(1, HOPS[s][d] + 1):
                ring(s, d, h).wait_send()
        for q in range(2):
            for h in range(1, 5):
                if a1_goes(q, d, h):
                    ring_a1(q, d, h).wait_send()
        for h in range(d, HOPS[B][d] + 1):
            over_y(d, h).wait_send()
        for which in (0, 1):
            col_x(d, which).wait_send()
        col_forward(d).wait_send()
    col_y().wait_send()
    for k in range(4):
        for which in (0, 1):
            col_c(which, k).wait_send()
    for j in range(4):
        for w in (0, 1):
            for dx in range(NX):
                out_copy(j, w, dx).wait()


def decode(code_ref, inst_ref, lag_ref):
    for w, ref in enumerate((inst_ref, lag_ref)):
        for k in range(code_ref.shape[0]):
            e = code_ref[k, w, W:CODE_ROWS, :].astype(jnp.float32)[:1]
            root = code_ref[k, w, :W, :].astype(jnp.float32) * (jnp.exp2(0.5 * e) / CODE_MAX)
            ref[k * W:(k + 1) * W, :] = root * jnp.abs(root)


def shards(frames, partner, usable):
    dma = pltpu.SemaphoreType.DMA
    blocks = frames.shape[1] // W
    out = jax.ShapeDtypeStruct((blocks, 2, CODE_ROWS, W), jnp.int16)
    anywhere = pl.BlockSpec(memory_space=pl.ANY)
    coded = pl.pallas_call(
        kernel,
        out_shape=out,
        in_specs=[anywhere] * 3,
        out_specs=anywhere,
        scratch_shapes=[
            pltpu.VMEM((BLOCKS, W), jnp.int32),
            pltpu.VMEM((BLOCKS, W), jnp.int32),
            pltpu.VMEM((64, 2048), jnp.bfloat16),
            pltpu.VMEM((NX, NZ, W, 512), jnp.bfloat16),
            pltpu.VMEM((FRAMES, 512), jnp.bfloat16),
            pltpu.VMEM((FRAMES, 512), jnp.bfloat16),
            pltpu.VMEM((FRAMES + W, 512), jnp.bfloat16),
            pltpu.VMEM((FRAMES, 1024), jnp.bfloat16),
            pltpu.VMEM((FRAMES, 2 * W), jnp.bfloat16),
            pltpu.VMEM((FRAMES, W), jnp.float32),
            pltpu.VMEM((FRAMES, W), jnp.float32),
            pltpu.VMEM((4, NX, 2, CODE_ROWS, W), jnp.int16),
            pltpu.VMEM((BLOCKS, W), jnp.float32),
            pltpu.VMEM((NZ, NL, 8, W), jnp.float32),
            pltpu.VMEM((4, NX, 8, W), jnp.float32),
            pltpu.VMEM((8, W), jnp.float32),
            pltpu.VMEM((4, 8, W), jnp.float32),
            dma((3,)), dma((2,)), dma((4,)), dma((4,)), dma((8,)), dma((8,)), dma((16,)), dma((16,)),
            dma((2, 2, 4)), dma((2, 2, 4)), dma((2, 2, 4)), dma((2, 2, 4)), dma((2, 5)), dma((2, 5)),
            dma((NZ, NL)), dma((NZ, NL)), dma((NX, 4)), dma((NX, 4)),
            dma(()), dma(()), dma((2, 2)), dma((2, 2)), dma((2,)), dma((2,)), dma((2, 4)), dma((2, 4)),
            dma((4, 2, NX)), dma((4, 2, NX)), dma((4, 2)),
        ],
        compiler_params=pltpu.CompilerParams(
            collective_id=0, has_side_effects=True, vmem_limit_bytes=56 << 20),
        name="covariances",
    )(partner.reshape(BLOCKS, W), usable.reshape(BLOCKS, W), frames)
    step = blocks // 2
    result = jax.ShapeDtypeStruct((blocks * W, W), jnp.float32)
    spec = pl.BlockSpec((step * W, W), lambda i: (i, 0))
    return pl.pallas_call(
        decode,
        grid=(blocks // step,),
        out_shape=(result, result),
        in_specs=[pl.BlockSpec((step, 2, CODE_ROWS, W), lambda i: (i, 0, 0, 0))],
        out_specs=(spec, spec),
        name="decode",
    )(coded)


def solution(mesh):
    in_specs = (P("tm", "tile"), P(), P())
    out_specs = (P("tile", "tm"), P("tile", "tm"))
    return jax.shard_map(shards, mesh=mesh, in_specs=in_specs, out_specs=out_specs, check_vma=False)
```
